256 devices in a mesh: section: 4 (over x), dp: 64 (over y, z, core).
Axes of the slice: x: 4, y: 4, z: 8, core: 2. Of those that a mesh axis runs over, the one named last changes fastest.
Arguments:
- section_inputs: bfloat16 [4, 8192, 4096], P('section', 'dp'), may hold values from -6 to 6
- gains: float32 [4, 4096], P('section'), may hold values from 0.25 to 1.75
- value_weight: bfloat16 [4, 4096, 1024], P('section', 'dp'), may hold values from -0.09375 to 0.09375
- top_cotangent: bfloat16 [8192, 4096], P('dp'), may hold values from -16 to 16
- proxy_loss: float32 [8192], P('dp'), may hold values from 0.5 to 5.5
- reference_loss: float32 [8192], P('dp'), may hold values from 1 to 3
- lengths: int32 [64, 8], P('dp'), may hold values from 1 to 80, 128 in all within a row
- doc_domain: int32 [64, 8], P('dp'), may hold values from 0 to 21
- log_weights: float32 [22], replicated, may hold values from -4 to -1
- step_count: int32 [1], replicated, may hold values from 1 to 256
Outputs:
- section_grads: bfloat16 [4, 8192, 4096], P('section', 'dp')
- weight_grads: float32 [4, 4096, 1024], P('section', 'dp')
- new_log_weights: float32 [22], replicated
The draws below stay inside these ranges and needn't reach their ends.
Inputs may be any that keep to these rules, and one draw needn't show every extreme that they name: `lengths`: each row sums to 128: the documents fill their pack in order.
All inputs are finite; a program needn't handle non-finite values.
Results may differ from the reference program's by a relative error of at most 0.0071.
Values may be sent and summed in bfloat16 or wider, within the bound.
No kernel may reach another device: no remote copies, remote signals or barrier semaphores. Data moves between devices by JAX's collectives and lax.ppermute only.
A program may use at most 128 MiB of HBM per device.

```python
import math
import jax
import jax.numpy as jnp
import numpy as np
from jax import lax

D = 4096
KV = 1024
DOMAINS = 22
DOCS = 8
TOK_DEV = 128
SECTIONS = 4
PACKS = 64
TOKENS = 8192
N_SECTION = 4
N_DP = 64


def draw_proxy_loss(key, part):
    position = jnp.arange(TOKENS, dtype=jnp.float32)
    spread = (1.0 + 2.0 * position / (TOKENS - 1)) / 3.0
    base = jax.random.uniform(key, (TOKENS,), jnp.float32)
    return 0.5 + 5.0 * base * spread


def plant(values, own_key, low, largest):
    longest = values.shape.index(max(values.shape))
    spots = []
    for shift in (0, 1):
        where = [jax.random.randint(jax.random.fold_in(own_key, axis), (), 0, length) for axis, length in enumerate(values.shape)]
        where[longest] = (where[longest] + shift) % values.shape[longest]
        spots.append(tuple(where))
    return values.at[spots[0]].set(low).at[spots[1]].set(largest)


def spiked(result, own_key, source, target, blocks, factor):
    def block_of(dim):
        return (jnp.arange(result.shape[dim]) // (result.shape[dim] // blocks)).reshape((-1,) + (1,) * (result.ndim - 1 - dim))

    near = jax.random.permutation(own_key, blocks)[block_of(target)]
    second = (block_of(target) + blocks // 2) % blocks
    return jnp.where((block_of(source) == near) | (block_of(source) == second), factor * result, result)


def block_scale(own_key, dims, shards, smallest, largest):
    loudness, own = 1.0, jax.random.fold_in(own_key, 6)
    for dim, blocks in shards:
        heights = jnp.exp(jax.random.uniform(jax.random.fold_in(own, dim), (blocks,), jnp.float32, smallest / len(shards), largest / len(shards)))
        loudness = loudness * jnp.repeat(heights, dims[dim] // blocks).reshape([-1 if axis == dim else 1 for axis in range(len(dims))])
    return loudness


def profile(number_of, total, most, slope):
    weights = [(1 << 20) // math.isqrt(standing ** slope) + 1 for standing in range(2, number_of + 1)]
    spare, given = total - most - (number_of - 1), [1] * (number_of - 1)
    while spare > 0:
        candidates = [i for i in range(number_of - 1) if given[i] < most]
        mass, budget = sum([weights[i] for i in candidates]), spare
        for i in candidates:
            addition = min(most - given[i], max(1, budget * weights[i] // mass), spare)
            given[i] = given[i] + addition
            spare = spare - addition
    return np.array([most] + given)


def uneven_parts(own_key, count, total, bound, lean):
    if count == 2:
        one = jax.random.randint(own_key, (), max(1, total - bound), min(bound, total - 1) + 1)
        return jnp.stack([one, total - one])
    sizes = jnp.asarray(profile(count, total, bound, lean), jnp.int32)
    twos = (count - 1) // 2
    giver, sink = sizes[1:1 + 2 * twos:2], sizes[2:2 + 2 * twos:2]
    slack = jnp.minimum(giver - 1, bound - sink)
    moved = jax.random.randint(jax.random.fold_in(own_key, 1), (twos,), 0, 1 << 20) % (slack + 1)
    sizes = sizes.at[1:1 + 2 * twos:2].set(giver - moved).at[2:2 + 2 * twos:2].set(sink + moved)
    return sizes[jax.random.permutation(jax.random.fold_in(own_key, 2), count)]


def bell_draw(rng, shape, scale, limit, split=(), held_as=jnp.bfloat16):
    entries = jax.random.normal(rng, shape, jnp.float32) * scale
    if len(split) > 0:
        entries = block_scale(rng, shape, split, -0.22, 0.18) * entries
    return jnp.clip(entries, min=-limit, max=limit).astype(held_as)


def heavy_noise(rng, shape, deviation, limit, cuts, heavy, kind=jnp.bfloat16):
    entries = deviation * jax.random.normal(rng, shape, jnp.float32)
    if cuts:
        entries = entries * block_scale(rng, shape, cuts, -0.22, 0.18)
    return jnp.clip(spiked(entries, jax.random.fold_in(rng, 3), *heavy), -limit, limit).astype(kind)


def setup_inputs(seed: int = 0) -> dict:
    streams_of = jax.random.split(jax.random.key(seed), 11)
    section_inputs = bell_draw(streams_of[0], (SECTIONS, TOKENS, D), 1.0, 6.0, ((0, 4), (1, 64)))
    gains = jnp.clip(1.0 + 0.15 * jax.random.normal(streams_of[1], (SECTIONS, D), jnp.float32), 0.25, 1.75)
    value_weight = bell_draw(streams_of[2], (SECTIONS, D, KV), D ** -0.5, 0.09375, ((0, 4), (1, 64)))
    top_cotangent = heavy_noise(streams_of[3], (TOKENS, D), 1.0, 16.0, ((0, 64),), (0, 1, 64, 4.0))
    proxy_loss = draw_proxy_loss(jax.random.fold_in(streams_of[10], 71), 0)
    reference_loss = jnp.clip(1.0 + 2.0 * jax.random.uniform(streams_of[5], (TOKENS,), jnp.float32) ** block_scale(streams_of[5], (TOKENS,), ((0, 64),), -0.2, 0.2), 1.0, 3.0)
    lengths = jax.vmap(lambda own: uneven_parts(own, DOCS, TOK_DEV, TOK_DEV // 2 + TOK_DEV // 8, 2))(jax.random.split(streams_of[6], PACKS)).reshape((PACKS, DOCS)).astype(jnp.int32)
    doc_domain = plant(jax.random.randint(streams_of[7], (PACKS, DOCS), 0, DOMAINS), jax.random.fold_in(streams_of[7], 1), 0, DOMAINS - 1).astype(jnp.int32)
    log_weights = jnp.clip(jax.random.uniform(streams_of[8], (DOMAINS,), jnp.float32, -4.0, -1.0), -4.0, -1.0)
    step_count = jax.random.randint(streams_of[9], (1,), 1, 257).astype(jnp.int32)
    return {"section_inputs": section_inputs, "gains": gains, "value_weight": value_weight, "top_cotangent": top_cotangent, "proxy_loss": proxy_loss, "reference_loss": reference_loss, "lengths": lengths, "doc_domain": doc_domain, "log_weights": log_weights, "step_count": step_count}


EPS = 1e-05
SMOOTH = 0.001

def token_weights(proxy_loss, reference_loss, lengths, doc_domain, log_weights, step_count):
    packs = lengths.shape[0]
    per_pack = proxy_loss.shape[0] // packs
    ends = jnp.cumsum(lengths, axis=1).astype(jnp.int32)
    position = jnp.arange(per_pack, dtype=jnp.int32)
    doc_index = lax.optimization_barrier(jnp.sum((position[None, :, None] >= ends[:, None, :]).astype(jnp.int32), axis=2))
    doc_hot = doc_index[:, :, None] == jnp.arange(DOCS, dtype=jnp.int32)[None, None, :]
    end_of = lax.optimization_barrier(jnp.sum(jnp.where(doc_hot, ends[:, None, :], 0), axis=2))
    live = (position[None, :] + 1 != end_of).reshape(-1)
    domain = lax.optimization_barrier(jnp.sum(jnp.where(doc_hot, doc_domain[:, None, :], 0), axis=2)).reshape(-1)
    onehot = (domain[:, None] == jnp.arange(DOMAINS, dtype=jnp.int32)[None, :]).astype(jnp.float32)
    selected = (live & (proxy_loss > reference_loss)).astype(jnp.float32)
    excess = selected * (proxy_loss - reference_loss)
    excess_sum = lax.optimization_barrier(jnp.sum(onehot * excess[:, None], axis=0))
    count = lax.optimization_barrier(jnp.sum(onehot * live.astype(jnp.float32)[:, None], axis=0))
    counts = jnp.maximum(count, 1.0)
    mean_excess = excess_sum / counts
    rate = 1.0 / jnp.sqrt(step_count[0].astype(jnp.float32))
    logits = log_weights + rate * mean_excess
    new_log = logits - jnp.log(jnp.sum(jnp.exp(logits)))
    lam = (1.0 - SMOOTH) * jnp.exp(new_log) + SMOOTH / DOMAINS
    per_domain = lam * proxy_loss.shape[0] / counts
    weight = lax.optimization_barrier(jnp.sum(onehot * per_domain[None, :], axis=1)) * selected
    return (weight, new_log)

def reference(section_inputs, gains, value_weight, top_cotangent, proxy_loss, reference_loss, lengths, doc_domain, log_weights, step_count):
    weight, new_log = token_weights(proxy_loss, reference_loss, lengths, doc_domain, log_weights, step_count)
    cotangent = top_cotangent
    grads_in = []
    grads_w = []
    for section in reversed(range(N_SECTION)):
        xfull = section_inputs[section].astype(jnp.float32)
        gamma = gains[section]
        projection = value_weight[section]
        inverse = lax.rsqrt(lax.optimization_barrier(jnp.mean(xfull * xfull, axis=1, keepdims=True)) + EPS)
        normed = (xfull * inverse * gamma[None, :]).astype(jnp.bfloat16)
        act = jnp.dot(normed, projection, preferred_element_type=jnp.float32)
        hidden = jax.nn.silu(act).astype(jnp.bfloat16)
        grad_h = jnp.dot(cotangent, projection, preferred_element_type=jnp.float32)
        sig = jax.nn.sigmoid(act)
        grad_a = grad_h * sig * (1.0 + act * (1.0 - sig))
        grad_n = jnp.dot(grad_a.astype(jnp.bfloat16), projection.T, preferred_element_type=jnp.float32)
        scaled = gamma[None, :] * grad_n
        grad_x = cotangent.astype(jnp.float32) + inverse * scaled - xfull * inverse ** 3 * lax.optimization_barrier(jnp.mean(xfull * scaled, axis=1, keepdims=True))
        passed = grad_x.astype(jnp.bfloat16)
        grads_in.append((weight[:, None] * passed.astype(jnp.float32)).astype(jnp.bfloat16))
        weighted_a = (weight[:, None] * grad_a).astype(jnp.bfloat16)
        weighted_g = (weight[:, None] * cotangent.astype(jnp.float32)).astype(jnp.bfloat16)
        total = jnp.dot(normed.T, weighted_a, preferred_element_type=jnp.float32) + jnp.dot(weighted_g.T, hidden, preferred_element_type=jnp.float32)
        grads_w.append(total / N_DP)
        cotangent = passed
    section_grads = jnp.stack(grads_in[::-1], axis=0)
    weight_grads = jnp.stack(grads_w[::-1], axis=0)
    return (section_grads, weight_grads, new_log)
```

```python
import jax
import jax.numpy as jnp
from jax import lax
from jax.sharding import Mesh
from jax.sharding import PartitionSpec as P

D = 4096
KV = 1024
DOMAINS = 22
MICRO = 4
DOCS = 8


EPS = 1e-05
SMOOTH = 0.001
Y, Z, CORE = 4, 8, 2
DP = ("y", "z", "core")


def shifted(value, axis, by):
    size = lax.axis_size(axis)
    return lax.ppermute(value, axis, [(i, (i + by) % size) for i in range(size)])


def flipped(value, axis, bit):
    size = lax.axis_size(axis)
    return lax.ppermute(value, axis, [(i, i ^ bit) for i in range(size)])


def summed(value):
    for axis, bits in (("core", (1,)), ("z", (1, 2, 4)), ("y", (1, 2))):
        for bit in bits:
            value = value + flipped(value, axis, bit)
    return value


def ring_scatter(blocks, axis):
    size, rows = blocks.shape[:2]
    here = lax.axis_index(axis)
    half = rows // 2

    def block(offset):
        return lax.dynamic_index_in_dim(blocks, (here + offset) % size, 0, keepdims=False)

    far = block(size // 2).astype(jnp.bfloat16)
    up = shifted(far[:half], axis, 1).astype(jnp.float32)
    down = shifted(far[half:], axis, -1).astype(jnp.float32)
    zero = jnp.zeros_like(up)
    up = jnp.concatenate([up, zero], axis=0)
    down = jnp.concatenate([zero, down], axis=0)
    for offset in range(size // 2 - 1, 0, -1):
        up = shifted((block(offset) + up).astype(jnp.bfloat16), axis, 1).astype(jnp.float32)
        down = shifted((block(-offset) + down).astype(jnp.bfloat16), axis, -1).astype(jnp.float32)
    return block(0) + up + down


def scattered(total):
    rows, cols = total.shape
    half = cols // 2
    unit = rows // (Y * Z)
    first = ring_scatter(total[:, :half].reshape(Y, Z * unit, half), "y")
    first = ring_scatter(first.reshape(Z, unit, half), "z")
    second = total[:, half:].reshape(Y, Z, unit, half).transpose(1, 0, 2, 3)
    second = ring_scatter(second.reshape(Z, Y * unit, half), "z")
    second = ring_scatter(second.reshape(Y, unit, half), "y")
    return jnp.concatenate([first, second], axis=1)


def passed_along(shard, axis, by):
    size = lax.axis_size(axis)
    pairs = [(i, i + by) for i in range(size) if 0 <= i + by < size]
    return lax.ppermute(shard, axis, pairs)


def local_statistics(proxy_loss, reference_loss, lengths, doc_domain):
    rows = proxy_loss.shape[0]
    ends = jnp.cumsum(lengths[0])
    position = jnp.arange(rows, dtype=jnp.int32)
    doc_index = jnp.sum((position[:, None] >= ends[None, :]).astype(jnp.int32), axis=1)
    doc_hot = doc_index[:, None] == jnp.arange(DOCS, dtype=jnp.int32)[None, :]
    end_of = jnp.sum(jnp.where(doc_hot, ends[None, :], 0), axis=1)
    live = position + 1 != end_of
    domain = jnp.sum(jnp.where(doc_hot, doc_domain[0][None, :], 0), axis=1)
    onehot = (domain[:, None] == jnp.arange(DOMAINS, dtype=jnp.int32)[None, :]).astype(jnp.float32)
    selected = (live & (proxy_loss > reference_loss)).astype(jnp.float32)
    excess = selected * (proxy_loss - reference_loss)
    excess_part = jnp.sum(onehot * excess[:, None], axis=0)
    count_part = jnp.sum(onehot * live.astype(jnp.float32)[:, None], axis=0)
    return (onehot, selected, excess_part, count_part)


def domain_weights(statistics, log_weights, step_count, total_tokens):
    onehot, selected, excess_part, count_part = statistics
    parts = jnp.zeros((2, 128), jnp.float32)
    parts = parts.at[0, :DOMAINS].set(excess_part).at[1, :DOMAINS].set(count_part)
    parts = summed(parts)
    excess_sum, count = parts[0, :DOMAINS], parts[1, :DOMAINS]
    counts = jnp.maximum(count, 1.0)
    mean_excess = excess_sum / counts
    rate = 1.0 / jnp.sqrt(step_count[0].astype(jnp.float32))
    logits = log_weights + rate * mean_excess
    new_log = logits - jnp.log(jnp.sum(jnp.exp(logits)))
    lam = (1.0 - SMOOTH) * jnp.exp(new_log) + SMOOTH / DOMAINS
    per_domain = lam * total_tokens / counts
    weight = jnp.sum(onehot * per_domain[None, :], axis=1) * selected
    return (weight, new_log)


def local(
    section_inputs,
    gains,
    value_weight,
    top_cotangent,
    proxy_loss,
    reference_loss,
    lengths,
    doc_domain,
    log_weights,
    step_count,
):
    sections = lax.axis_size("section")
    section = lax.axis_index("section")
    devices = Y * Z * CORE
    core = lax.axis_index("core")
    mine = core * (KV // 2)
    other = (1 - core) * (KV // 2)
    xfull = section_inputs[0].astype(jnp.float32)
    gamma = gains[0]
    shard = value_weight[0]
    rows = xfull.shape[0]
    block = rows // MICRO
    total_tokens = rows * devices
    statistics = local_statistics(proxy_loss, reference_loss, lengths, doc_domain)
    weight, new_log = domain_weights(statistics, log_weights, step_count, total_tokens)
    inverse = lax.rsqrt(jnp.mean(xfull * xfull, axis=1, keepdims=True) + EPS)
    normed = (xfull * inverse * gamma[None, :]).astype(jnp.bfloat16)
    full_weight = lax.all_gather(shard, DP, axis=0, tiled=True)
    act = jnp.dot(normed, full_weight, preferred_element_type=jnp.float32)
    hidden = jax.nn.silu(act).astype(jnp.bfloat16)
    kept_cot = jnp.zeros((rows, D), jnp.bfloat16)
    kept_da = jnp.zeros((rows, KV), jnp.float32)
    kept_dx = jnp.zeros((rows, D), jnp.bfloat16)
    state = (kept_cot, kept_da, kept_dx)
    received = jnp.zeros((block, D), jnp.bfloat16)
    ticks = MICRO + sections - 1
    for tick in range(ticks):
        index = tick - (sections - 1) + section
        active = (index >= 0) & (index < MICRO)
        start = jnp.clip(index, 0, MICRO - 1) * block
        top = lax.dynamic_slice_in_dim(top_cotangent, start, block, 0)
        incoming = jnp.where(section == sections - 1, top, received)

        def work(current):
            cot_buf, da_buf, dx_buf = current
            act_part = lax.dynamic_slice_in_dim(act, start, block, 0)
            x_part = lax.dynamic_slice_in_dim(xfull, start, block, 0)
            scale = lax.dynamic_slice_in_dim(inverse, start, block, 0)
            grad_h = jnp.einsum(
                "td,dk->tk", incoming, full_weight, preferred_element_type=jnp.float32
            )
            sig = jax.nn.sigmoid(act_part)
            grad_a = grad_h * sig * (1.0 + act_part * (1.0 - sig))
            grad_n = jnp.einsum(
                "tk,dk->td",
                grad_a.astype(jnp.bfloat16),
                full_weight,
                preferred_element_type=jnp.float32,
            )
            scaled = gamma[None, :] * grad_n
            grad_x = (
                incoming.astype(jnp.float32)
                + scale * scaled
                - x_part * scale**3 * jnp.mean(x_part * scaled, axis=1, keepdims=True)
            )
            passed = grad_x.astype(jnp.bfloat16)
            cot_buf = lax.dynamic_update_slice_in_dim(cot_buf, incoming, start, 0)
            da_buf = lax.dynamic_update_slice_in_dim(da_buf, grad_a, start, 0)
            dx_buf = lax.dynamic_update_slice_in_dim(dx_buf, passed, start, 0)
            return ((cot_buf, da_buf, dx_buf), passed)

        def skip(current):
            return (current, jnp.zeros((block, D), jnp.bfloat16))

        state, outgoing = lax.cond(active, work, skip, state)
        if tick + 1 < ticks:
            received = passed_along(outgoing, "section", -1)
    kept_cot, kept_da, kept_dx = state
    section_grad = (weight[:, None] * kept_dx.astype(jnp.float32)).astype(jnp.bfloat16)
    weighted_a = (weight[:, None] * kept_da).astype(jnp.bfloat16)
    weighted_g = (weight[:, None] * kept_cot.astype(jnp.float32)).astype(jnp.bfloat16)
    left = jnp.concatenate([normed, weighted_g], axis=0)
    right = jnp.concatenate([weighted_a, hidden], axis=0)
    theirs = lax.dynamic_slice_in_dim(right, other, KV // 2, 1)
    ours = lax.dynamic_slice_in_dim(right, mine, KV // 2, 1)
    left = jnp.concatenate([left, shifted(left, "core", 1)], axis=0)
    right = jnp.concatenate([ours, shifted(theirs, "core", 1)], axis=0)
    total = jnp.einsum("td,tk->dk", left, right, preferred_element_type=jnp.float32)
    part = scattered(total / devices)
    size = part.shape[0] // 2
    kept = lax.dynamic_slice_in_dim(part, core * size, size, 0)
    sent = lax.dynamic_slice_in_dim(part, (1 - core) * size, size, 0)
    got = shifted(sent, "core", 1)
    grad_shard = jnp.where(
        core == 0,
        jnp.concatenate([kept, got], axis=1),
        jnp.concatenate([got, kept], axis=1),
    )
    return (section_grad[None], grad_shard[None], new_log)


def solution(mesh):
    grid = Mesh(mesh.devices.reshape(-1, Y, Z, CORE), ("section",) + DP)
    return jax.shard_map(
        local,
        mesh=grid,
        in_specs=(
            P("section", DP, None),
            P("section", None),
            P("section", DP, None),
            P(DP, None),
            P(DP),
            P(DP),
            P(DP, None),
            P(DP, None),
            P(),
            P(),
        ),
        out_specs=(P("section", DP, None), P("section", DP, None), P()),
        check_vma=False,
    )
```

```python
import functools

import jax
import jax.numpy as jnp
from jax import lax
from jax.experimental import pallas as pl
from jax.experimental.pallas import tpu as pltpu
from jax.sharding import Mesh
from jax.sharding import PartitionSpec as P

D = 4096
KV = 1024
DOMAINS = 22
MICRO = 4
SECTIONS = 4
DOCS = 8


EPS = 1e-05
SMOOTH = 0.001
Y, Z, CORE = 4, 8, 2
STEP = 512
LAG = 3
VMEM_LIMIT = 24 * 1024 * 1024


DP = ("y", "z", "core")


def shifted(value, axis, by):
    size = lax.axis_size(axis)
    return lax.ppermute(value, axis, [(i, (i + by) % size) for i in range(size)])


def flipped(value, axis, bit):
    size = lax.axis_size(axis)
    return lax.ppermute(value, axis, [(i, i ^ bit) for i in range(size)])


def summed(value):
    for axis, bits in (("core", (1,)), ("z", (1, 2, 4)), ("y", (1, 2))):
        for bit in bits:
            value = value + flipped(value, axis, bit)
    return value


def ring_scatter(blocks, axis):
    size, rows = blocks.shape[:2]
    here = lax.axis_index(axis)
    half = rows // 2

    def block(offset):
        return lax.dynamic_index_in_dim(blocks, (here + offset) % size, 0, keepdims=False)

    far = block(size // 2).astype(jnp.bfloat16)
    up = shifted(far[:half], axis, 1).astype(jnp.float32)
    down = shifted(far[half:], axis, -1).astype(jnp.float32)
    zero = jnp.zeros_like(up)
    up = jnp.concatenate([up, zero], axis=0)
    down = jnp.concatenate([zero, down], axis=0)
    for offset in range(size // 2 - 1, 0, -1):
        up = shifted((block(offset) + up).astype(jnp.bfloat16), axis, 1).astype(jnp.float32)
        down = shifted((block(-offset) + down).astype(jnp.bfloat16), axis, -1).astype(jnp.float32)
    return block(0) + up + down


def scattered(total):
    rows, cols = total.shape
    half = cols // 2
    unit = rows // (Y * Z)
    first = ring_scatter(total[:, :half].reshape(Y, Z * unit, half), "y")
    first = ring_scatter(first.reshape(Z, unit, half), "z")
    second = total[:, half:].reshape(Y, Z, unit, half).transpose(1, 0, 2, 3)
    second = ring_scatter(second.reshape(Z, Y * unit, half), "z")
    second = ring_scatter(second.reshape(Y, unit, half), "y")
    return jnp.concatenate([first, second], axis=1)


def local_statistics(proxy_loss, reference_loss, lengths, doc_domain):
    rows = proxy_loss.shape[0]
    ends = jnp.cumsum(lengths[0])
    position = jnp.arange(rows, dtype=jnp.int32)
    doc_index = jnp.sum((position[:, None] >= ends[None, :]).astype(jnp.int32), axis=1)
    doc_hot = doc_index[:, None] == jnp.arange(DOCS, dtype=jnp.int32)[None, :]
    end_of = jnp.sum(jnp.where(doc_hot, ends[None, :], 0), axis=1)
    live = position + 1 != end_of
    domain = jnp.sum(jnp.where(doc_hot, doc_domain[0][None, :], 0), axis=1)
    onehot = (domain[:, None] == jnp.arange(DOMAINS, dtype=jnp.int32)[None, :]).astype(jnp.float32)
    selected = (live & (proxy_loss > reference_loss)).astype(jnp.float32)
    excess = selected * (proxy_loss - reference_loss)
    excess_part = jnp.sum(onehot * excess[:, None], axis=0)
    count_part = jnp.sum(onehot * live.astype(jnp.float32)[:, None], axis=0)
    return (onehot, selected, excess_part, count_part)


def domain_weights(statistics, log_weights, step_count, total_tokens):
    onehot, selected, excess_part, count_part = statistics
    parts = jnp.zeros((2, 128), jnp.float32)
    parts = parts.at[0, :DOMAINS].set(excess_part).at[1, :DOMAINS].set(count_part)
    parts = summed(parts)
    excess_sum, count = parts[0, :DOMAINS], parts[1, :DOMAINS]
    counts = jnp.maximum(count, 1.0)
    mean_excess = excess_sum / counts
    rate = 1.0 / jnp.sqrt(step_count[0].astype(jnp.float32))
    logits = log_weights + rate * mean_excess
    new_log = logits - jnp.log(jnp.sum(jnp.exp(logits)))
    lam = (1.0 - SMOOTH) * jnp.exp(new_log) + SMOOTH / DOMAINS
    per_domain = lam * total_tokens / counts
    weight = jnp.sum(onehot * per_domain[None, :], axis=1) * selected
    return (weight, new_log)


def forward_kernel(x_ref, r_ref, gamma_ref, w_ref, normed_ref, slope_ref, hidden_ref):
    depth = x_ref.shape[1]
    step = min(STEP, depth)
    slope_ref[...] = jnp.zeros_like(slope_ref)

    @pl.loop(0, depth // step)
    def _(i):
        cols = pl.ds(pl.multiple_of(i * step, step), step)
        x = x_ref[:, cols].astype(jnp.float32)
        normed = (x * r_ref[...] * gamma_ref[:, cols]).astype(jnp.bfloat16)
        normed_ref[:, cols] = normed
        slope_ref[...] += jnp.dot(normed, w_ref[cols, :], preferred_element_type=jnp.float32)

    act = slope_ref[...]
    sig = jax.nn.sigmoid(act)
    hidden_ref[...] = (act * sig).astype(jnp.bfloat16)
    slope_ref[...] = sig * (1.0 + act * (1.0 - sig))


def forward(x, inverse, gamma, weight):
    rows, depth = x.shape
    width = weight.shape[1]
    spec = pl.BlockSpec(memory_space=pltpu.VMEM)
    return pl.pallas_call(
        forward_kernel,
        in_specs=[spec] * 4,
        out_specs=[spec] * 3,
        out_shape=[
            jax.ShapeDtypeStruct((rows, depth), jnp.bfloat16),
            jax.ShapeDtypeStruct((rows, width), jnp.float32),
            jax.ShapeDtypeStruct((rows, width), jnp.bfloat16),
        ],
        compiler_params=pltpu.CompilerParams(vmem_limit_bytes=VMEM_LIMIT),
        cost_estimate=pl.CostEstimate(
            flops=2 * rows * depth * width, bytes_accessed=2 * depth * width, transcendentals=0
        ),
        name="forward",
    )(x, inverse, gamma, weight)


def tick_kernel(
    slot,
    section_ref,
    came_ref,
    top_ref,
    x_ref,
    r_ref,
    weight_ref,
    slope_ref,
    gamma_ref,
    w_ref,
    old_dx_ref,
    old_wg_ref,
    old_wa_ref,
    out_ref,
    dx_ref,
    wg_ref,
    wa_ref,
    cot_ref,
    acc_ref,
    scaled_ref,
):
    depth = x_ref.shape[1]
    step = min(STEP, depth)
    index = slot - LAG * (SECTIONS - 1 - section_ref[0])
    active = (index >= 0) & (index < MICRO)
    is_top = section_ref[0] == SECTIONS - 1

    @pl.when(jnp.logical_not(active))
    def _():
        dx_ref[...] = old_dx_ref[...]
        wg_ref[...] = old_wg_ref[...]
        wa_ref[...] = old_wa_ref[...]

    @pl.when(active)
    def _():
        @pl.when(is_top)
        def _():
            cot_ref[...] = top_ref[...]

        @pl.when(jnp.logical_not(is_top))
        def _():
            cot_ref[...] = came_ref[...]

        acc_ref[...] = jnp.zeros_like(acc_ref)

        @pl.loop(0, depth // step)
        def _(i):
            cols = pl.ds(pl.multiple_of(i * step, step), step)
            acc_ref[...] += jnp.dot(
                cot_ref[:, cols], w_ref[cols, :], preferred_element_type=jnp.float32
            )

        grad_a = acc_ref[...] * slope_ref[...]
        wa_ref[...] = (weight_ref[...] * grad_a).astype(jnp.bfloat16)
        rounded = grad_a.astype(jnp.bfloat16)

        def back(i, dots):
            cols = pl.ds(pl.multiple_of(i * step, step), step)
            grad_n = lax.dot_general(
                rounded,
                w_ref[cols, :],
                (((1,), (1,)), ((), ())),
                preferred_element_type=jnp.float32,
            )
            scaled = gamma_ref[:, cols] * grad_n
            scaled_ref[:, cols] = scaled
            prod = x_ref[:, cols].astype(jnp.float32) * scaled
            return dots + jnp.sum(prod, axis=1, keepdims=True)

        dots = lax.fori_loop(
            0, depth // step, back, jnp.zeros((x_ref.shape[0], 1), jnp.float32)
        )
        r = r_ref[...]
        pull = r * r * r * (dots / depth)
        weight = weight_ref[...]

        @pl.loop(0, depth // step)
        def _(i):
            cols = pl.ds(pl.multiple_of(i * step, step), step)
            cot = cot_ref[:, cols].astype(jnp.float32)
            x = x_ref[:, cols].astype(jnp.float32)
            passed = (cot + r * scaled_ref[:, cols] - x * pull).astype(jnp.bfloat16)
            out_ref[:, cols] = passed
            dx_ref[:, cols] = (weight * passed.astype(jnp.float32)).astype(jnp.bfloat16)
            wg_ref[:, cols] = (weight * cot).astype(jnp.bfloat16)


def tick(slot, section, came, top, x, inverse, weight, slope, gamma, w, dx, wg, wa):
    block, depth = came.shape
    width = slope.shape[1]

    def place(section):
        return jnp.clip(slot - LAG * (SECTIONS - 1 - section), 0, MICRO - 1)

    def rows(cols):
        return pl.BlockSpec((block, cols), lambda i, section: (place(section[0]), 0))

    def whole(shape):
        return pl.BlockSpec(shape, lambda i, section: (0, 0))

    return pl.pallas_call(
        functools.partial(tick_kernel, slot),
        grid_spec=pltpu.PrefetchScalarGridSpec(
            num_scalar_prefetch=1,
            grid=(1,),
            in_specs=[
                whole((block, depth)),
                rows(depth),
                rows(depth),
                rows(1),
                rows(1),
                rows(width),
                whole((1, depth)),
                pl.BlockSpec(memory_space=pltpu.VMEM),
                rows(depth),
                rows(depth),
                rows(width),
            ],
            out_specs=[whole((block, depth)), rows(depth), rows(depth), rows(width)],
            scratch_shapes=[
                pltpu.VMEM((block, depth), jnp.bfloat16),
                pltpu.VMEM((block, width), jnp.float32),
                pltpu.VMEM((block, depth), jnp.float32),
            ],
        ),
        out_shape=[
            jax.ShapeDtypeStruct((block, depth), jnp.bfloat16),
            jax.ShapeDtypeStruct(dx.shape, dx.dtype),
            jax.ShapeDtypeStruct(wg.shape, wg.dtype),
            jax.ShapeDtypeStruct(wa.shape, wa.dtype),
        ],
        input_output_aliases={9: 1, 10: 2, 11: 3},
        compiler_params=pltpu.CompilerParams(vmem_limit_bytes=VMEM_LIMIT),
        cost_estimate=pl.CostEstimate(
            flops=4 * 128 * depth * width, bytes_accessed=2 * depth * width, transcendentals=0
        ),
        name="tick",
    )(section, came, top, x, inverse, weight, slope, gamma, w, dx, wg, wa)


def local(
    section_inputs,
    gains,
    value_weight,
    top_cotangent,
    proxy_loss,
    reference_loss,
    lengths,
    doc_domain,
    log_weights,
    step_count,
):
    sections = lax.axis_size("section")
    section = lax.axis_index("section").astype(jnp.int32)[None]
    devices = Y * Z * CORE
    core = lax.axis_index("core")
    x = section_inputs[0]
    shard = value_weight[0]
    rows, depth = x.shape
    width = shard.shape[1]
    mine = core * (width // 2)
    other = (1 - core) * (width // 2)
    block = rows // MICRO
    total_tokens = rows * devices
    statistics = local_statistics(proxy_loss, reference_loss, lengths, doc_domain)
    weight, new_log = domain_weights(statistics, log_weights, step_count, total_tokens)
    weight = weight[:, None]
    xfull = x.astype(jnp.float32)
    inverse = lax.rsqrt(jnp.mean(xfull * xfull, axis=1, keepdims=True) + EPS)
    inverse, weight = lax.optimization_barrier((inverse, weight))
    full_weight = lax.all_gather(shard, DP, axis=0, tiled=True)
    normed, slope, hidden = forward(x, inverse, gains, full_weight)
    dx = jnp.zeros((rows, depth), jnp.bfloat16)
    wg = jnp.zeros((rows, depth), jnp.bfloat16)
    wa = jnp.zeros((rows, width), jnp.bfloat16)
    sent = {}
    ticks = MICRO + LAG * (sections - 1)
    for slot in range(ticks):
        came = sent[slot - LAG] if slot >= LAG else jnp.zeros((block, depth), jnp.bfloat16)
        out, dx, wg, wa = tick(
            slot,
            section,
            came,
            top_cotangent,
            x,
            inverse,
            weight,
            slope,
            gains,
            full_weight,
            dx,
            wg,
            wa,
        )
        pairs = [
            (s, s - 1)
            for s in range(1, sections)
            if 0 <= slot - LAG * (sections - 1 - s) < MICRO
        ]
        if pairs:
            sent[slot] = lax.ppermute(out, "section", pairs)
    left = jnp.concatenate([normed, wg], axis=0)
    right = jnp.concatenate([wa, hidden], axis=0)
    theirs = lax.dynamic_slice_in_dim(right, other, width // 2, 1)
    ours = lax.dynamic_slice_in_dim(right, mine, width // 2, 1)
    left = jnp.concatenate([left, shifted(left, "core", 1)], axis=0)
    right = jnp.concatenate([ours, shifted(theirs, "core", 1)], axis=0)
    total = jnp.einsum("td,tk->dk", left, right, preferred_element_type=jnp.float32)
    part = scattered(total / devices)
    size = part.shape[0] // 2
    kept = lax.dynamic_slice_in_dim(part, core * size, size, 0)
    leaving = lax.dynamic_slice_in_dim(part, (1 - core) * size, size, 0)
    got = shifted(leaving, "core", 1)
    grad_shard = jnp.where(
        core == 0,
        jnp.concatenate([kept, got], axis=1),
        jnp.concatenate([got, kept], axis=1),
    )
    return (dx[None], grad_shard[None], new_log)


def solution(mesh):
    grid = Mesh(mesh.devices.reshape(-1, Y, Z, CORE), ("section",) + DP)
    return jax.shard_map(
        local,
        mesh=grid,
        in_specs=(
            P("section", DP, None),
            P("section", None),
            P("section", DP, None),
            P(DP, None),
            P(DP),
            P(DP),
            P(DP, None),
            P(DP, None),
            P(),
            P(),
        ),
        out_specs=(P("section", DP, None), P("section", DP, None), P()),
        check_vma=False,
    )
```

```python
import functools

import jax
import jax.numpy as jnp
from jax import lax
from jax.experimental import pallas as pl
from jax.experimental.pallas import tpu as pltpu
from jax.sharding import Mesh
from jax.sharding import PartitionSpec as P

D = 4096
KV = 1024
DOMAINS = 22
MICRO = 4
SECTIONS = 4
DOCS = 8


EPS = 1e-05
SMOOTH = 0.001
Y, Z, CORE = 4, 8, 2
STEP = 1024
STEP_IN = 1024
STEP_OUT = 1024
STEP_END = 512
LAG = 3
VMEM_LIMIT = 24 * 1024 * 1024


DP = ("y", "z", "core")


def shifted(value, axis, by):
    size = lax.axis_size(axis)
    return lax.ppermute(value, axis, [(i, (i + by) % size) for i in range(size)])


def flipped(value, axis, bit):
    size = lax.axis_size(axis)
    return lax.ppermute(value, axis, [(i, i ^ bit) for i in range(size)])


def summed(value):
    for axis, bits in (("core", (1,)), ("z", (1, 2, 4)), ("y", (1, 2))):
        for bit in bits:
            value = value + flipped(value, axis, bit)
    return value


def ring_scatter(blocks, axis):
    size, rows = blocks.shape[:2]
    here = lax.axis_index(axis)
    half = rows // 2

    def block(offset):
        return lax.dynamic_index_in_dim(blocks, (here + offset) % size, 0, keepdims=False)

    far = block(size // 2).astype(jnp.bfloat16)
    up = shifted(far[:half], axis, 1).astype(jnp.float32)
    down = shifted(far[half:], axis, -1).astype(jnp.float32)
    zero = jnp.zeros_like(up)
    up = jnp.concatenate([up, zero], axis=0)
    down = jnp.concatenate([zero, down], axis=0)
    for offset in range(size // 2 - 1, 0, -1):
        up = shifted((block(offset) + up).astype(jnp.bfloat16), axis, 1).astype(jnp.float32)
        down = shifted((block(-offset) + down).astype(jnp.bfloat16), axis, -1).astype(jnp.float32)
    return block(0) + up + down


def scattered(total):
    rows, cols = total.shape
    half = cols // 2
    unit = rows // (Y * Z)
    first = ring_scatter(total[:, :half].reshape(Y, Z * unit, half), "y")
    first = ring_scatter(first.reshape(Z, unit, half), "z")
    second = total[:, half:].reshape(Y, Z, unit, half).transpose(1, 0, 2, 3)
    second = ring_scatter(second.reshape(Z, Y * unit, half), "z")
    second = ring_scatter(second.reshape(Y, unit, half), "y")
    return jnp.concatenate([first, second], axis=1)


def local_statistics(proxy_loss, reference_loss, lengths, doc_domain):
    rows = proxy_loss.shape[0]
    ends = jnp.cumsum(lengths[0])
    position = jnp.arange(rows, dtype=jnp.int32)
    doc_index = jnp.sum((position[:, None] >= ends[None, :]).astype(jnp.int32), axis=1)
    doc_hot = doc_index[:, None] == jnp.arange(DOCS, dtype=jnp.int32)[None, :]
    end_of = jnp.sum(jnp.where(doc_hot, ends[None, :], 0), axis=1)
    live = position + 1 != end_of
    domain = jnp.sum(jnp.where(doc_hot, doc_domain[0][None, :], 0), axis=1)
    onehot = (domain[:, None] == jnp.arange(DOMAINS, dtype=jnp.int32)[None, :]).astype(jnp.float32)
    selected = (live & (proxy_loss > reference_loss)).astype(jnp.float32)
    excess = selected * (proxy_loss - reference_loss)
    excess_part = jnp.sum(onehot * excess[:, None], axis=0)
    count_part = jnp.sum(onehot * live.astype(jnp.float32)[:, None], axis=0)
    return (onehot, selected, excess_part, count_part)


def domain_weights(statistics, log_weights, step_count, total_tokens):
    onehot, selected, excess_part, count_part = statistics
    parts = jnp.zeros((2, 128), jnp.float32)
    parts = parts.at[0, :DOMAINS].set(excess_part).at[1, :DOMAINS].set(count_part)
    parts = summed(parts)
    excess_sum, count = parts[0, :DOMAINS], parts[1, :DOMAINS]
    counts = jnp.maximum(count, 1.0)
    mean_excess = excess_sum / counts
    rate = 1.0 / jnp.sqrt(step_count[0].astype(jnp.float32))
    logits = log_weights + rate * mean_excess
    new_log = logits - jnp.log(jnp.sum(jnp.exp(logits)))
    lam = (1.0 - SMOOTH) * jnp.exp(new_log) + SMOOTH / DOMAINS
    per_domain = lam * total_tokens / counts
    weight = jnp.sum(onehot * per_domain[None, :], axis=1) * selected
    return (weight, new_log)


def forward_kernel(x_ref, r_ref, gamma_ref, w_ref, normed_ref, slope_ref, hidden_ref):
    depth = x_ref.shape[1]
    step = min(STEP, depth)
    slope_ref[...] = jnp.zeros_like(slope_ref)

    @pl.loop(0, depth // step)
    def _(i):
        cols = pl.ds(pl.multiple_of(i * step, step), step)
        x = x_ref[:, cols].astype(jnp.float32)
        normed = (x * r_ref[...] * gamma_ref[:, cols]).astype(jnp.bfloat16)
        normed_ref[:, cols] = normed
        slope_ref[...] += jnp.dot(normed, w_ref[cols, :], preferred_element_type=jnp.float32)

    act = slope_ref[...]
    sig = jax.nn.sigmoid(act)
    hidden_ref[...] = (act * sig).astype(jnp.bfloat16)
    slope_ref[...] = sig * (1.0 + act * (1.0 - sig))


def forward(x, inverse, gamma, weight):
    rows, depth = x.shape
    width = weight.shape[1]
    spec = pl.BlockSpec(memory_space=pltpu.VMEM)
    return pl.pallas_call(
        forward_kernel,
        in_specs=[spec] * 4,
        out_specs=[spec] * 3,
        out_shape=[
            jax.ShapeDtypeStruct((rows, depth), jnp.bfloat16),
            jax.ShapeDtypeStruct((rows, width), jnp.float32),
            jax.ShapeDtypeStruct((rows, width), jnp.bfloat16),
        ],
        compiler_params=pltpu.CompilerParams(vmem_limit_bytes=VMEM_LIMIT),
        cost_estimate=pl.CostEstimate(
            flops=2 * rows * depth * width, bytes_accessed=2 * depth * width, transcendentals=0
        ),
        name="forward",
    )(x, inverse, gamma, weight)


def tick_kernel(
    index_ref,
    section_ref,
    came_ref,
    top_ref,
    x_ref,
    r_ref,
    weight_ref,
    slope_ref,
    gamma_ref,
    w_ref,
    old_dx_ref,
    old_wg_ref,
    old_wa_ref,
    out_ref,
    dx_ref,
    wg_ref,
    wa_ref,
    cot_ref,
    scaled_ref,
    dx_block,
    wg_block,
    wa_block,
    sems,
):
    block, depth = came_ref.shape
    index = index_ref[0]
    is_top = section_ref[0] == SECTIONS - 1

    @pl.when((index >= 0) & (index < MICRO))
    def _():
        rows = pl.ds(pl.multiple_of(index * block, block), block)

        @pl.when(is_top)
        def _():
            cot_ref[...] = top_ref[rows, :]

        @pl.when(jnp.logical_not(is_top))
        def _():
            cot_ref[...] = came_ref[...]

        weight = weight_ref[rows, :]
        wg_block[...] = (weight * cot_ref[...].astype(jnp.float32)).astype(jnp.bfloat16)
        wg_copy = pltpu.make_async_copy(wg_block, wg_ref.at[rows, :], sems.at[0])
        wg_copy.start()
        grad_h = jnp.zeros((block, w_ref.shape[1]), jnp.float32)
        step = min(STEP_IN, depth)
        for i in range(depth // step):
            cols = pl.ds(i * step, step)
            grad_h += jnp.dot(
                cot_ref[:, cols], w_ref[cols, :], preferred_element_type=jnp.float32
            )
        grad_a = grad_h * slope_ref[rows, :]
        wa_block[...] = (weight * grad_a).astype(jnp.bfloat16)
        wa_copy = pltpu.make_async_copy(wa_block, wa_ref.at[rows, :], sems.at[1])
        wa_copy.start()
        rounded = grad_a.astype(jnp.bfloat16)
        dots = jnp.zeros((block, 1), jnp.float32)
        step = min(STEP_OUT, depth)
        for i in range(depth // step):
            cols = pl.ds(i * step, step)
            grad_n = lax.dot_general(
                rounded,
                w_ref[cols, :],
                (((1,), (1,)), ((), ())),
                preferred_element_type=jnp.float32,
            )
            scaled = gamma_ref[:, cols] * grad_n
            scaled_ref[:, cols] = scaled
            prod = x_ref[rows, cols].astype(jnp.float32) * scaled
            dots += jnp.sum(prod, axis=1, keepdims=True)
        r = r_ref[rows, :]
        pull = r * r * r * (dots / depth)
        step = min(STEP_END, depth)
        for i in range(depth // step):
            cols = pl.ds(i * step, step)
            cot = cot_ref[:, cols].astype(jnp.float32)
            x = x_ref[rows, cols].astype(jnp.float32)
            passed = (cot + r * scaled_ref[:, cols] - x * pull).astype(jnp.bfloat16)
            out_ref[:, cols] = passed
            dx_block[:, cols] = (weight * passed.astype(jnp.float32)).astype(jnp.bfloat16)
        dx_copy = pltpu.make_async_copy(dx_block, dx_ref.at[rows, :], sems.at[2])
        dx_copy.start()
        wg_copy.wait()
        wa_copy.wait()
        dx_copy.wait()


def tick(index, section, came, top, x, inverse, weight, slope, gamma, w, dx, wg, wa):
    block, depth = came.shape
    width = slope.shape[1]
    spec = pl.BlockSpec(memory_space=pltpu.VMEM)
    scalar = pl.BlockSpec(memory_space=pltpu.SMEM)
    return pl.pallas_call(
        tick_kernel,
        in_specs=[scalar] * 2 + [spec] * 8 + [pl.BlockSpec(memory_space=pl.ANY)] * 3,
        out_specs=[spec] + [pl.BlockSpec(memory_space=pl.ANY)] * 3,
        scratch_shapes=[
            pltpu.VMEM((block, depth), jnp.bfloat16),
            pltpu.VMEM((block, depth), jnp.float32),
            pltpu.VMEM((block, depth), jnp.bfloat16),
            pltpu.VMEM((block, depth), jnp.bfloat16),
            pltpu.VMEM((block, width), jnp.bfloat16),
            pltpu.SemaphoreType.DMA((3,)),
        ],
        out_shape=[
            jax.ShapeDtypeStruct((block, depth), jnp.bfloat16),
            jax.ShapeDtypeStruct(dx.shape, dx.dtype),
            jax.ShapeDtypeStruct(wg.shape, wg.dtype),
            jax.ShapeDtypeStruct(wa.shape, wa.dtype),
        ],
        input_output_aliases={10: 1, 11: 2, 12: 3},
        compiler_params=pltpu.CompilerParams(vmem_limit_bytes=VMEM_LIMIT),
        cost_estimate=pl.CostEstimate(
            flops=4 * 128 * depth * width, bytes_accessed=2 * depth * width, transcendentals=0
        ),
        name="tick",
    )(index, section, came, top, x, inverse, weight, slope, gamma, w, dx, wg, wa)


def local(
    section_inputs,
    gains,
    value_weight,
    top_cotangent,
    proxy_loss,
    reference_loss,
    lengths,
    doc_domain,
    log_weights,
    step_count,
):
    sections = lax.axis_size("section")
    section = lax.axis_index("section").astype(jnp.int32)[None]
    devices = Y * Z * CORE
    core = lax.axis_index("core")
    x = section_inputs[0]
    shard = value_weight[0]
    rows, depth = x.shape
    width = shard.shape[1]
    mine = core * (width // 2)
    other = (1 - core) * (width // 2)
    block = rows // MICRO
    total_tokens = rows * devices
    statistics = local_statistics(proxy_loss, reference_loss, lengths, doc_domain)
    weight, new_log = domain_weights(statistics, log_weights, step_count, total_tokens)
    weight = weight[:, None]
    xfull = x.astype(jnp.float32)
    inverse = lax.rsqrt(jnp.mean(xfull * xfull, axis=1, keepdims=True) + EPS)
    inverse, weight = lax.optimization_barrier((inverse, weight))
    full_weight = lax.all_gather(shard, DP, axis=0, tiled=True)
    normed, slope, hidden = forward(x, inverse, gains, full_weight)
    dx = jnp.zeros((rows, depth), jnp.bfloat16)
    wg = jnp.zeros((rows, depth), jnp.bfloat16)
    wa = jnp.zeros((rows, width), jnp.bfloat16)
    sent = {}
    ticks = MICRO + LAG * (sections - 1)
    for slot in range(ticks):
        came = sent[slot - LAG] if slot >= LAG else jnp.zeros((block, depth), jnp.bfloat16)
        out, dx, wg, wa = tick(
            section + (slot - LAG * (sections - 1)) + (LAG - 1) * section,
            section,
            came,
            top_cotangent,
            x,
            inverse,
            weight,
            slope,
            gains,
            full_weight,
            dx,
            wg,
            wa,
        )
        pairs = [
            (s, s - 1)
            for s in range(1, sections)
            if 0 <= slot - LAG * (sections - 1 - s) < MICRO
        ]
        if pairs:
            sent[slot] = lax.ppermute(out, "section", pairs)
    left = jnp.concatenate([normed, wg], axis=0)
    right = jnp.concatenate([wa, hidden], axis=0)
    theirs = lax.dynamic_slice_in_dim(right, other, width // 2, 1)
    ours = lax.dynamic_slice_in_dim(right, mine, width // 2, 1)
    left = jnp.concatenate([left, shifted(left, "core", 1)], axis=0)
    right = jnp.concatenate([ours, shifted(theirs, "core", 1)], axis=0)
    total = jnp.einsum("td,tk->dk", left, right, preferred_element_type=jnp.float32)
    part = scattered(total / devices)
    size = part.shape[0] // 2
    kept = lax.dynamic_slice_in_dim(part, core * size, size, 0)
    leaving = lax.dynamic_slice_in_dim(part, (1 - core) * size, size, 0)
    got = shifted(leaving, "core", 1)
    grad_shard = jnp.where(
        core == 0,
        jnp.concatenate([kept, got], axis=1),
        jnp.concatenate([got, kept], axis=1),
    )
    return (dx[None], grad_shard[None], new_log)


def solution(mesh):
    grid = Mesh(mesh.devices.reshape(-1, Y, Z, CORE), ("section",) + DP)
    return jax.shard_map(
        local,
        mesh=grid,
        in_specs=(
            P("section", DP, None),
            P("section", None),
            P("section", DP, None),
            P(DP, None),
            P(DP),
            P(DP),
            P(DP, None),
            P(DP, None),
            P(),
            P(),
        ),
        out_specs=(P("section", DP, None), P("section", DP, None), P()),
        check_vma=False,
    )
```

```python
import jax
import jax.numpy as jnp
from jax import lax
from jax.experimental import pallas as pl
from jax.experimental.pallas import tpu as pltpu
from jax.sharding import Mesh
from jax.sharding import PartitionSpec as P

DOMAINS = 22
MICRO = 4
SECTIONS = 4
DOCS = 8


EPS = 1e-05
SMOOTH = 0.001
Y, Z, CORE = 4, 8, 2
STEP = 1024
STEP_IN = 2048
STEP_OUT = 2048
STEP_END = 512
LAG = 3
VMEM_LIMIT = 24 * 1024 * 1024


DP = ("y", "z", "core")


def shifted(value, axis, by):
    size = lax.axis_size(axis)
    return lax.ppermute(value, axis, [(i, (i + by) % size) for i in range(size)])


def summed(value):
    for axis in ("core", "z", "y"):
        size = lax.axis_size(axis)
        copies = jnp.broadcast_to(value[None], (size,) + value.shape)
        value = jnp.sum(lax.all_to_all(copies, axis, 0, 0, tiled=True), axis=0)
    return value


def ring_scatter(block, size, axis):
    def pair(high, low):
        high, low = lax.optimization_barrier(
            (high.astype(jnp.bfloat16), low.astype(jnp.bfloat16))
        )
        high, low = shifted(high, axis, 1), shifted(low, axis, -1)
        return high.astype(jnp.float32), low.astype(jnp.float32)

    far = block(size // 2)
    half = far.shape[0] // 2
    up, down = pair(far[:half], far[half:])
    zero = jnp.zeros_like(up)
    up = jnp.concatenate([up, zero], axis=0)
    down = jnp.concatenate([zero, down], axis=0)
    for offset in range(size // 2 - 1, 0, -1):
        up, down = pair(block(offset) + up, block(-offset) + down)
    return block(0) + up + down


def swapped(blocks, axis):
    got = lax.all_to_all(blocks.astype(jnp.bfloat16), axis, 0, 0, tiled=True)
    total = got[0].astype(jnp.float32)
    for i in range(1, got.shape[0]):
        total = total + got[i].astype(jnp.float32)
    return total


def scattered(left, right):
    depth, cols = left.shape[1], right.shape[1]
    half = cols // 2
    unit = depth // (Y * Z)
    first = jnp.einsum("td,tk->dk", left, right[:, :half], preferred_element_type=jnp.float32)
    first = first.astype(jnp.bfloat16)
    later, first = lax.optimization_barrier((right[:, half:], first))
    first = swapped(first.reshape(Y, Z * unit, half), "y")
    second = jnp.einsum("td,tk->dk", left, later, preferred_element_type=jnp.float32)
    second = second.reshape(Y, Z, unit, half)
    here = lax.axis_index("z")

    def block(offset):
        piece = lax.dynamic_slice_in_dim(second, (here + offset) % Z, 1, 1)
        return piece.reshape(Y * unit, half)

    second = ring_scatter(block, Z, "z")
    first = swapped(first.reshape(Z, unit, half), "z")
    second = swapped(second.reshape(Y, unit, half), "y")
    return jnp.concatenate([first, second], axis=1)


def local_statistics(proxy_loss, reference_loss, lengths, doc_domain):
    rows = proxy_loss.shape[0]
    ends = jnp.cumsum(lengths[0])
    position = jnp.arange(rows, dtype=jnp.int32)
    doc_index = jnp.sum((position[:, None] >= ends[None, :]).astype(jnp.int32), axis=1)
    doc_hot = doc_index[:, None] == jnp.arange(DOCS, dtype=jnp.int32)[None, :]
    end_of = jnp.sum(jnp.where(doc_hot, ends[None, :], 0), axis=1)
    live = position + 1 != end_of
    domain = jnp.sum(jnp.where(doc_hot, doc_domain[0][None, :], 0), axis=1)
    onehot = (domain[:, None] == jnp.arange(DOMAINS, dtype=jnp.int32)[None, :]).astype(jnp.float32)
    selected = (live & (proxy_loss > reference_loss)).astype(jnp.float32)
    excess = selected * (proxy_loss - reference_loss)
    excess_part = jnp.sum(onehot * excess[:, None], axis=0)
    count_part = jnp.sum(onehot * live.astype(jnp.float32)[:, None], axis=0)
    return (onehot, selected, excess_part, count_part)


def domain_weights(statistics, log_weights, step_count, total_tokens):
    onehot, selected, excess_part, count_part = statistics
    parts = jnp.zeros((8, 128), jnp.float32)
    parts = parts.at[0, :DOMAINS].set(excess_part).at[1, :DOMAINS].set(count_part)
    parts = summed(parts)
    excess_sum, count = parts[0, :DOMAINS], parts[1, :DOMAINS]
    counts = jnp.maximum(count, 1.0)
    mean_excess = excess_sum / counts
    rate = 1.0 / jnp.sqrt(step_count[0].astype(jnp.float32))
    logits = log_weights + rate * mean_excess
    new_log = logits - jnp.log(jnp.sum(jnp.exp(logits)))
    lam = (1.0 - SMOOTH) * jnp.exp(new_log) + SMOOTH / DOMAINS
    per_domain = lam * total_tokens / counts
    weight = jnp.sum(onehot * per_domain[None, :], axis=1) * selected
    return (weight, new_log)


def forward_kernel(x_ref, r_ref, gamma_ref, w_ref, normed_ref, slope_ref, hidden_ref):
    depth = x_ref.shape[1]
    step = min(STEP, depth)
    slope_ref[...] = jnp.zeros_like(slope_ref)

    @pl.loop(0, depth // step)
    def _(i):
        cols = pl.ds(pl.multiple_of(i * step, step), step)
        x = x_ref[:, cols].astype(jnp.float32)
        normed = (x * r_ref[...] * gamma_ref[:, cols]).astype(jnp.bfloat16)
        normed_ref[:, cols] = normed
        slope_ref[...] += jnp.dot(normed, w_ref[cols, :], preferred_element_type=jnp.float32)

    act = slope_ref[...]
    sig = jax.nn.sigmoid(act)
    hidden_ref[...] = (act * sig).astype(jnp.bfloat16)
    slope_ref[...] = sig * (1.0 + act * (1.0 - sig))


def forward(x, inverse, gamma, weight):
    rows, depth = x.shape
    width = weight.shape[1]
    spec = pl.BlockSpec(memory_space=pltpu.VMEM)
    return pl.pallas_call(
        forward_kernel,
        in_specs=[spec] * 4,
        out_specs=[spec] * 3,
        out_shape=[
            jax.ShapeDtypeStruct((rows, depth), jnp.bfloat16),
            jax.ShapeDtypeStruct((rows, width), jnp.float32),
            jax.ShapeDtypeStruct((rows, width), jnp.bfloat16),
        ],
        compiler_params=pltpu.CompilerParams(vmem_limit_bytes=VMEM_LIMIT),
        cost_estimate=pl.CostEstimate(
            flops=2 * rows * depth * width, bytes_accessed=2 * depth * width, transcendentals=0
        ),
        name="forward",
    )(x, inverse, gamma, weight)


def tick_kernel(
    index_ref,
    section_ref,
    came_ref,
    top_ref,
    x_ref,
    r_ref,
    weight_ref,
    slope_ref,
    gamma_ref,
    w_ref,
    old_dx_ref,
    old_wg_ref,
    old_wa_ref,
    out_ref,
    dx_ref,
    wg_ref,
    wa_ref,
    cot_ref,
    scaled_ref,
    dx_block,
    wg_block,
    wa_block,
    sems,
):
    block, depth = came_ref.shape
    index = index_ref[0]
    is_top = section_ref[0] == SECTIONS - 1

    @pl.when((index >= 0) & (index < MICRO))
    def _():
        rows = pl.ds(pl.multiple_of(index * block, block), block)

        @pl.when(is_top)
        def _():
            cot_ref[...] = top_ref[rows, :]

        @pl.when(jnp.logical_not(is_top))
        def _():
            cot_ref[...] = came_ref[...]

        weight = weight_ref[rows, :]
        wg_block[...] = (weight * cot_ref[...].astype(jnp.float32)).astype(jnp.bfloat16)
        wg_copy = pltpu.make_async_copy(wg_block, wg_ref.at[rows, :], sems.at[0])
        wg_copy.start()
        step = min(STEP_IN, depth)

        def into(i, total):
            cols = pl.ds(pl.multiple_of(i * step, step), step)
            return total + jnp.dot(
                cot_ref[:, cols], w_ref[cols, :], preferred_element_type=jnp.float32
            )

        grad_h = lax.fori_loop(
            0, depth // step, into, jnp.zeros((block, w_ref.shape[1]), jnp.float32)
        )
        grad_a = grad_h * slope_ref[rows, :]
        wa_block[...] = (weight * grad_a).astype(jnp.bfloat16)
        wa_copy = pltpu.make_async_copy(wa_block, wa_ref.at[rows, :], sems.at[1])
        wa_copy.start()
        rounded = grad_a.astype(jnp.bfloat16)
        stride = min(STEP_OUT, depth)

        def back(i, dots):
            cols = pl.ds(pl.multiple_of(i * stride, stride), stride)
            grad_n = lax.dot_general(
                rounded,
                w_ref[cols, :],
                (((1,), (1,)), ((), ())),
                preferred_element_type=jnp.float32,
            )
            scaled = gamma_ref[:, cols] * grad_n
            scaled_ref[:, cols] = scaled
            prod = x_ref[rows, cols].astype(jnp.float32) * scaled
            return dots + jnp.sum(prod, axis=1, keepdims=True)

        dots = lax.fori_loop(0, depth // stride, back, jnp.zeros((block, 1), jnp.float32))
        r = r_ref[rows, :]
        pull = r * r * r * (dots / depth)
        span = min(STEP_END, depth)

        @pl.loop(0, depth // span)
        def _(i):
            cols = pl.ds(pl.multiple_of(i * span, span), span)
            cot = cot_ref[:, cols].astype(jnp.float32)
            x = x_ref[rows, cols].astype(jnp.float32)
            passed = (cot + r * scaled_ref[:, cols] - x * pull).astype(jnp.bfloat16)
            out_ref[:, cols] = passed
            dx_block[:, cols] = (weight * passed.astype(jnp.float32)).astype(jnp.bfloat16)

        dx_copy = pltpu.make_async_copy(dx_block, dx_ref.at[rows, :], sems.at[2])
        dx_copy.start()
        wg_copy.wait()
        wa_copy.wait()
        dx_copy.wait()


def tick(index, section, came, top, x, inverse, weight, slope, gamma, w, dx, wg, wa):
    block, depth = came.shape
    width = slope.shape[1]
    spec = pl.BlockSpec(memory_space=pltpu.VMEM)
    scalar = pl.BlockSpec(memory_space=pltpu.SMEM)
    return pl.pallas_call(
        tick_kernel,
        in_specs=[scalar] * 2 + [spec] * 8 + [pl.BlockSpec(memory_space=pl.ANY)] * 3,
        out_specs=[spec] + [pl.BlockSpec(memory_space=pl.ANY)] * 3,
        scratch_shapes=[
            pltpu.VMEM((block, depth), jnp.bfloat16),
            pltpu.VMEM((block, depth), jnp.float32),
            pltpu.VMEM((block, depth), jnp.bfloat16),
            pltpu.VMEM((block, depth), jnp.bfloat16),
            pltpu.VMEM((block, width), jnp.bfloat16),
            pltpu.SemaphoreType.DMA((3,)),
        ],
        out_shape=[
            jax.ShapeDtypeStruct((block, depth), jnp.bfloat16),
            jax.ShapeDtypeStruct(dx.shape, dx.dtype),
            jax.ShapeDtypeStruct(wg.shape, wg.dtype),
            jax.ShapeDtypeStruct(wa.shape, wa.dtype),
        ],
        input_output_aliases={10: 1, 11: 2, 12: 3},
        compiler_params=pltpu.CompilerParams(vmem_limit_bytes=VMEM_LIMIT),
        cost_estimate=pl.CostEstimate(
            flops=4 * 128 * depth * width, bytes_accessed=2 * depth * width, transcendentals=0
        ),
        name="tick",
    )(index, section, came, top, x, inverse, weight, slope, gamma, w, dx, wg, wa)


def local(
    section_inputs,
    gains,
    value_weight,
    top_cotangent,
    proxy_loss,
    reference_loss,
    lengths,
    doc_domain,
    log_weights,
    step_count,
):
    sections = lax.axis_size("section")
    section = lax.axis_index("section").astype(jnp.int32)[None]
    devices = Y * Z * CORE
    core = lax.axis_index("core")
    x = section_inputs[0]
    shard = value_weight[0]
    rows, depth = x.shape
    width = shard.shape[1]
    block = rows // MICRO
    total_tokens = rows * devices
    statistics = local_statistics(proxy_loss, reference_loss, lengths, doc_domain)
    weight, new_log = domain_weights(statistics, log_weights, step_count, total_tokens)
    weight = weight[:, None]
    xfull = x.astype(jnp.float32)
    inverse = lax.rsqrt(jnp.mean(xfull * xfull, axis=1, keepdims=True) + EPS)
    inverse, weight = lax.optimization_barrier((inverse, weight))
    full_weight = lax.all_gather(shard, DP, axis=0, tiled=True)
    normed, slope, hidden = forward(x, inverse, gains, full_weight)
    dx = jnp.zeros((rows, depth), jnp.bfloat16)
    wg = jnp.zeros((rows, depth), jnp.bfloat16)
    wa = jnp.zeros((rows, width), jnp.bfloat16)
    sent = {}
    ticks = MICRO + LAG * (sections - 1)
    for slot in range(ticks):
        came = sent[slot - LAG] if slot >= LAG else jnp.zeros((block, depth), jnp.bfloat16)
        out, dx, wg, wa = tick(
            section + (slot - LAG * (sections - 1)) + (LAG - 1) * section,
            section,
            came,
            top_cotangent,
            x,
            inverse,
            weight,
            slope,
            gains,
            full_weight,
            dx,
            wg,
            wa,
        )
        pairs = [
            (s, s - 1)
            for s in range(1, sections)
            if 0 <= slot - LAG * (sections - 1 - s) < MICRO
        ]
        if pairs:
            sent[slot] = lax.ppermute(out, "section", pairs)
    left = jnp.concatenate([normed, wg], axis=0)
    right = jnp.concatenate([wa, hidden], axis=0)
    left = jnp.concatenate([left, shifted(left, "core", 1)], axis=0)
    halves = right.reshape(2 * rows, CORE, width // CORE).transpose(1, 0, 2)
    halves = lax.all_to_all(halves, "core", 0, 0, tiled=True)
    order = jnp.where(core == 0, halves, halves[::-1])
    right = order.reshape(CORE * 2 * rows, width // CORE)
    part = scattered(left, right) * (1.0 / devices)
    pieces = lax.all_to_all(part.reshape(CORE, -1, width // CORE), "core", 0, 0, tiled=True)
    grad_shard = pieces.transpose(1, 0, 2).reshape(shard.shape)
    return (dx[None], grad_shard[None], new_log)


def solution(mesh):
    grid = Mesh(mesh.devices.reshape(-1, Y, Z, CORE), ("section",) + DP)
    return jax.shard_map(
        local,
        mesh=grid,
        in_specs=(
            P("section", DP, None),
            P("section", None),
            P("section", DP, None),
            P(DP, None),
            P(DP),
            P(DP),
            P(DP, None),
            P(DP, None),
            P(),
            P(),
        ),
        out_specs=(P("section", DP, None), P("section", DP, None), P()),
        check_vma=False,
    )
```

```python
import jax
import jax.numpy as jnp
from jax import lax
from jax.experimental import pallas as pl
from jax.experimental.pallas import tpu as pltpu
from jax.sharding import Mesh
from jax.sharding import PartitionSpec as P

DOMAINS = 22
MICRO = 4
SECTIONS = 4
DOCS = 8


EPS = 1e-05
SMOOTH = 0.001
Y, Z, CORE = 4, 8, 2
STEP = 1024
STEP_IN = 2048
STEP_OUT = 2048
STEP_END = 512
LAG = 3
VMEM_LIMIT = 24 * 1024 * 1024


DP = ("y", "z", "core")


def shifted(value, axis, by):
    size = lax.axis_size(axis)
    return lax.ppermute(value, axis, [(i, (i + by) % size) for i in range(size)])


def ring_scatter(block, size, axis):
    def pair(high, low):
        high, low = lax.optimization_barrier(
            (high.astype(jnp.bfloat16), low.astype(jnp.bfloat16))
        )
        high, low = shifted(high, axis, 1), shifted(low, axis, -1)
        return high.astype(jnp.float32), low.astype(jnp.float32)

    far = block(size // 2)
    half = far.shape[0] // 2
    up, down = pair(far[:half], far[half:])
    zero = jnp.zeros_like(up)
    up = jnp.concatenate([up, zero], axis=0)
    down = jnp.concatenate([zero, down], axis=0)
    for offset in range(size // 2 - 1, 0, -1):
        up, down = pair(block(offset) + up, block(-offset) + down)
    return block(0) + up + down


def spread(block, axis):
    size = lax.axis_size(axis)
    copies = jnp.broadcast_to(block[None], (size,) + block.shape)
    return lax.all_to_all(copies, axis, 0, 0, tiled=True)


SUMS = (("core", 1), ("z", 1), ("z", 2), ("z", 4), ("y", 1), ("y", 2))


def ring_gather(block, value, axis):
    size = lax.axis_size(axis)
    pieces = {0: block}
    half = block.shape[0] // 2
    up = down = block
    for offset in range(1, size // 2 + 1):
        last = offset == size // 2
        if last:
            up, down = up[:half], down[half:]
        up, down, value = lax.optimization_barrier((up, down, value))
        up, down = shifted(up, axis, 1), shifted(down, axis, -1)
        for name, bit in SUMS[2 * offset - 2 : 2 * offset]:
            pairs = [(i, i ^ bit) for i in range(lax.axis_size(name))]
            value = value + lax.ppermute(value, name, pairs)
        if not last:
            pieces[-offset], pieces[offset] = up, down
    pieces[size // 2] = jnp.concatenate([up, down], axis=0)
    return pieces, value


def gathered(shard, value):
    rows, width = shard.shape
    half = width // CORE
    cut = half // 2
    chip = shard.reshape(rows, CORE, half).transpose(1, 0, 2)
    chip = lax.all_to_all(chip, "core", 0, 0, tiled=True).reshape(CORE * rows, half)
    unit = CORE * rows
    slim, rest = chip[:, :cut], chip[:, cut:]
    slim = spread(slim, "y")
    slim, rest = lax.optimization_barrier((slim, rest))
    pieces, value = ring_gather(slim.reshape(Y * unit, cut), value, "z")
    wide = spread(rest, "z")
    wide = spread(wide.reshape(Z * unit, half - cut), "y")
    here = lax.axis_index("z")
    own = jnp.zeros((Y, Z, unit, cut), jnp.bfloat16)
    for offset, piece in pieces.items():
        piece = piece.reshape(Y, 1, unit, cut)
        own = lax.dynamic_update_slice_in_dim(own, piece, (here + offset) % Z, 1)
    own = jnp.concatenate([own.reshape(-1, cut), wide.reshape(-1, half - cut)], axis=1)
    return jnp.concatenate([own, shifted(own, "core", 1)], axis=1), value


def swapped(blocks, axis):
    got = lax.all_to_all(blocks.astype(jnp.bfloat16), axis, 0, 0, tiled=True)
    total = got[0].astype(jnp.float32)
    for i in range(1, got.shape[0]):
        total = total + got[i].astype(jnp.float32)
    return total


def scattered(left, right):
    depth, cols = left.shape[1], right.shape[1]
    half = cols // 2
    unit = depth // (Y * Z)
    first = jnp.einsum("td,tk->dk", left, right[:, :half], preferred_element_type=jnp.float32)
    first = first.astype(jnp.bfloat16)
    later, first = lax.optimization_barrier((right[:, half:], first))
    first = swapped(first.reshape(Y, Z * unit, half), "y")
    second = jnp.einsum("td,tk->dk", left, later, preferred_element_type=jnp.float32)
    second = second.reshape(Y, Z, unit, half)
    here = lax.axis_index("z")

    def block(offset):
        piece = lax.dynamic_slice_in_dim(second, (here + offset) % Z, 1, 1)
        return piece.reshape(Y * unit, half)

    second = ring_scatter(block, Z, "z")
    first = swapped(first.reshape(Z, unit, half), "z")
    first, second = lax.optimization_barrier((first, second))
    second = swapped(second.reshape(Y, unit, half), "y")
    return jnp.concatenate([first, second], axis=1)


def local_statistics(proxy_loss, reference_loss, lengths, doc_domain):
    rows = proxy_loss.shape[0]
    ends = jnp.cumsum(lengths[0])
    position = jnp.arange(rows, dtype=jnp.int32)
    doc_index = jnp.sum((position[:, None] >= ends[None, :]).astype(jnp.int32), axis=1)
    doc_hot = doc_index[:, None] == jnp.arange(DOCS, dtype=jnp.int32)[None, :]
    end_of = jnp.sum(jnp.where(doc_hot, ends[None, :], 0), axis=1)
    live = position + 1 != end_of
    domain = jnp.sum(jnp.where(doc_hot, doc_domain[0][None, :], 0), axis=1)
    onehot = (domain[:, None] == jnp.arange(DOMAINS, dtype=jnp.int32)[None, :]).astype(jnp.float32)
    selected = (live & (proxy_loss > reference_loss)).astype(jnp.float32)
    excess = selected * (proxy_loss - reference_loss)
    excess_part = jnp.sum(onehot * excess[:, None], axis=0)
    count_part = jnp.sum(onehot * live.astype(jnp.float32)[:, None], axis=0)
    return (onehot, selected, excess_part, count_part)


def domain_weights(statistics, parts, log_weights, step_count, total_tokens):
    onehot, selected = statistics[:2]
    excess_sum, count = parts[0, :DOMAINS], parts[1, :DOMAINS]
    counts = jnp.maximum(count, 1.0)
    mean_excess = excess_sum / counts
    rate = 1.0 / jnp.sqrt(step_count[0].astype(jnp.float32))
    logits = log_weights + rate * mean_excess
    new_log = logits - jnp.log(jnp.sum(jnp.exp(logits)))
    lam = (1.0 - SMOOTH) * jnp.exp(new_log) + SMOOTH / DOMAINS
    per_domain = lam * total_tokens / counts
    weight = jnp.sum(onehot * per_domain[None, :], axis=1) * selected
    return (weight, new_log)


def forward_kernel(x_ref, r_ref, gamma_ref, w_ref, normed_ref, slope_ref, hidden_ref):
    depth = x_ref.shape[1]
    step = min(STEP, depth)
    slope_ref[...] = jnp.zeros_like(slope_ref)

    @pl.loop(0, depth // step)
    def _(i):
        cols = pl.ds(pl.multiple_of(i * step, step), step)
        x = x_ref[:, cols].astype(jnp.float32)
        normed = (x * r_ref[...] * gamma_ref[:, cols]).astype(jnp.bfloat16)
        normed_ref[:, cols] = normed
        slope_ref[...] += jnp.dot(normed, w_ref[cols, :], preferred_element_type=jnp.float32)

    act = slope_ref[...]
    sig = jax.nn.sigmoid(act)
    hidden_ref[...] = (act * sig).astype(jnp.bfloat16)
    slope_ref[...] = sig * (1.0 + act * (1.0 - sig))


def forward(x, inverse, gamma, weight):
    rows, depth = x.shape
    width = weight.shape[1]
    spec = pl.BlockSpec(memory_space=pltpu.VMEM)
    return pl.pallas_call(
        forward_kernel,
        in_specs=[spec] * 4,
        out_specs=[spec] * 3,
        out_shape=[
            jax.ShapeDtypeStruct((rows, depth), jnp.bfloat16),
            jax.ShapeDtypeStruct((rows, width), jnp.float32),
            jax.ShapeDtypeStruct((rows, width), jnp.bfloat16),
        ],
        compiler_params=pltpu.CompilerParams(vmem_limit_bytes=VMEM_LIMIT),
        cost_estimate=pl.CostEstimate(
            flops=2 * rows * depth * width, bytes_accessed=2 * depth * width, transcendentals=0
        ),
        name="forward",
    )(x, inverse, gamma, weight)


def tick_kernel(
    index_ref,
    section_ref,
    came_ref,
    top_ref,
    x_ref,
    r_ref,
    weight_ref,
    slope_ref,
    gamma_ref,
    w_ref,
    old_dx_ref,
    old_wg_ref,
    old_wa_ref,
    out_ref,
    dx_ref,
    wg_ref,
    wa_ref,
    cot_ref,
    scaled_ref,
    dx_block,
    wg_block,
    wa_block,
    sems,
):
    block, depth = came_ref.shape
    index = index_ref[0]
    is_top = section_ref[0] == SECTIONS - 1

    @pl.when((index >= 0) & (index < MICRO))
    def _():
        rows = pl.ds(pl.multiple_of(index * block, block), block)

        @pl.when(is_top)
        def _():
            cot_ref[...] = top_ref[rows, :]

        @pl.when(jnp.logical_not(is_top))
        def _():
            cot_ref[...] = came_ref[...]

        weight = weight_ref[rows, :]
        wg_block[...] = (weight * cot_ref[...].astype(jnp.float32)).astype(jnp.bfloat16)
        wg_copy = pltpu.make_async_copy(wg_block, wg_ref.at[rows, :], sems.at[0])
        wg_copy.start()
        step = min(STEP_IN, depth)

        def into(i, total):
            cols = pl.ds(pl.multiple_of(i * step, step), step)
            return total + jnp.dot(
                cot_ref[:, cols], w_ref[cols, :], preferred_element_type=jnp.float32
            )

        grad_h = lax.fori_loop(
            0, depth // step, into, jnp.zeros((block, w_ref.shape[1]), jnp.float32)
        )
        grad_a = grad_h * slope_ref[rows, :]
        wa_block[...] = (weight * grad_a).astype(jnp.bfloat16)
        wa_copy = pltpu.make_async_copy(wa_block, wa_ref.at[rows, :], sems.at[1])
        wa_copy.start()
        rounded = grad_a.astype(jnp.bfloat16)
        stride = min(STEP_OUT, depth)

        def back(i, dots):
            cols = pl.ds(pl.multiple_of(i * stride, stride), stride)
            grad_n = lax.dot_general(
                rounded,
                w_ref[cols, :],
                (((1,), (1,)), ((), ())),
                preferred_element_type=jnp.float32,
            )
            scaled = gamma_ref[:, cols] * grad_n
            scaled_ref[:, cols] = scaled
            prod = x_ref[rows, cols].astype(jnp.float32) * scaled
            return dots + jnp.sum(prod, axis=1, keepdims=True)

        dots = lax.fori_loop(0, depth // stride, back, jnp.zeros((block, 1), jnp.float32))
        r = r_ref[rows, :]
        pull = r * r * r * (dots / depth)
        span = min(STEP_END, depth)

        @pl.loop(0, depth // span)
        def _(i):
            cols = pl.ds(pl.multiple_of(i * span, span), span)
            cot = cot_ref[:, cols].astype(jnp.float32)
            x = x_ref[rows, cols].astype(jnp.float32)
            passed = (cot + r * scaled_ref[:, cols] - x * pull).astype(jnp.bfloat16)
            out_ref[:, cols] = passed
            dx_block[:, cols] = (weight * passed.astype(jnp.float32)).astype(jnp.bfloat16)

        dx_copy = pltpu.make_async_copy(dx_block, dx_ref.at[rows, :], sems.at[2])
        dx_copy.start()
        wg_copy.wait()
        wa_copy.wait()
        dx_copy.wait()


def tick(index, section, came, top, x, inverse, weight, slope, gamma, w, dx, wg, wa):
    block, depth = came.shape
    width = slope.shape[1]
    spec = pl.BlockSpec(memory_space=pltpu.VMEM)
    scalar = pl.BlockSpec(memory_space=pltpu.SMEM)
    return pl.pallas_call(
        tick_kernel,
        in_specs=[scalar] * 2 + [spec] * 8 + [pl.BlockSpec(memory_space=pl.ANY)] * 3,
        out_specs=[spec] + [pl.BlockSpec(memory_space=pl.ANY)] * 3,
        scratch_shapes=[
            pltpu.VMEM((block, depth), jnp.bfloat16),
            pltpu.VMEM((block, depth), jnp.float32),
            pltpu.VMEM((block, depth), jnp.bfloat16),
            pltpu.VMEM((block, depth), jnp.bfloat16),
            pltpu.VMEM((block, width), jnp.bfloat16),
            pltpu.SemaphoreType.DMA((3,)),
        ],
        out_shape=[
            jax.ShapeDtypeStruct((block, depth), jnp.bfloat16),
            jax.ShapeDtypeStruct(dx.shape, dx.dtype),
            jax.ShapeDtypeStruct(wg.shape, wg.dtype),
            jax.ShapeDtypeStruct(wa.shape, wa.dtype),
        ],
        input_output_aliases={10: 1, 11: 2, 12: 3},
        compiler_params=pltpu.CompilerParams(vmem_limit_bytes=VMEM_LIMIT),
        cost_estimate=pl.CostEstimate(
            flops=4 * 128 * depth * width, bytes_accessed=2 * depth * width, transcendentals=0
        ),
        name="tick",
    )(index, section, came, top, x, inverse, weight, slope, gamma, w, dx, wg, wa)


def local(
    section_inputs,
    gains,
    value_weight,
    top_cotangent,
    proxy_loss,
    reference_loss,
    lengths,
    doc_domain,
    log_weights,
    step_count,
):
    sections = lax.axis_size("section")
    section = lax.axis_index("section").astype(jnp.int32)[None]
    devices = Y * Z * CORE
    x = section_inputs[0]
    shard = value_weight[0]
    rows, depth = x.shape
    width = shard.shape[1]
    block = rows // MICRO
    total_tokens = rows * devices
    statistics = local_statistics(proxy_loss, reference_loss, lengths, doc_domain)
    parts = jnp.zeros((8, 128), jnp.float32)
    parts = parts.at[0, :DOMAINS].set(statistics[2]).at[1, :DOMAINS].set(statistics[3])
    full_weight, parts = gathered(shard, parts)
    weight, new_log = domain_weights(statistics, parts, log_weights, step_count, total_tokens)
    weight = weight[:, None]
    xfull = x.astype(jnp.float32)
    inverse = lax.rsqrt(jnp.mean(xfull * xfull, axis=1, keepdims=True) + EPS)
    normed, slope, hidden = forward(x, inverse, gains, full_weight)
    dx = jnp.zeros((rows, depth), jnp.bfloat16)
    wg = jnp.zeros((rows, depth), jnp.bfloat16)
    wa = jnp.zeros((rows, width), jnp.bfloat16)
    sent = {}
    ticks = MICRO + LAG * (sections - 1)
    for slot in range(ticks):
        came = sent[slot - LAG] if slot >= LAG else jnp.zeros((block, depth), jnp.bfloat16)
        out, dx, wg, wa = tick(
            section + (slot - LAG * (sections - 1)) + (LAG - 1) * section,
            section,
            came,
            top_cotangent,
            x,
            inverse,
            weight,
            slope,
            gains,
            full_weight,
            dx,
            wg,
            wa,
        )
        pairs = [
            (s, s - 1)
            for s in range(1, sections)
            if 0 <= slot - LAG * (sections - 1 - s) < MICRO
        ]
        if pairs:
            sent[slot] = lax.ppermute(out, "section", pairs)
    left = jnp.concatenate([normed, wg], axis=0)
    right = jnp.concatenate([wa, hidden], axis=0)
    left = jnp.concatenate([left, shifted(left, "core", 1)], axis=0)
    half = width // CORE
    right = jnp.concatenate([right[:, :half], shifted(right[:, half:], "core", 1)], axis=0)
    part = scattered(left, right) * (1.0 / devices)
    pieces = lax.all_to_all(part.reshape(CORE, -1, width // CORE), "core", 0, 0, tiled=True)
    grad_shard = pieces.transpose(1, 0, 2).reshape(shard.shape)
    return (dx[None], grad_shard[None], new_log)


def solution(mesh):
    grid = Mesh(mesh.devices.reshape(-1, Y, Z, CORE), ("section",) + DP)
    return jax.shard_map(
        local,
        mesh=grid,
        in_specs=(
            P("section", DP, None),
            P("section", None),
            P("section", DP, None),
            P(DP, None),
            P(DP),
            P(DP),
            P(DP, None),
            P(DP, None),
            P(),
            P(),
        ),
        out_specs=(P("section", DP, None), P("section", DP, None), P()),
        check_vma=False,
    )
```

```python
import jax
import jax.numpy as jnp
from jax import lax
from jax.experimental import pallas as pl
from jax.experimental.pallas import tpu as pltpu
from jax.sharding import Mesh
from jax.sharding import PartitionSpec as P

DOMAINS = 22
MICRO = 4
SECTIONS = 4
DOCS = 8


EPS = 1e-05
SMOOTH = 0.001
Y, Z, CORE = 4, 8, 2
STEP = 1024
STEP_IN = 2048
STEP_OUT = 2048
STEP_END = 512
LAG = 2
VMEM_LIMIT = 24 * 1024 * 1024


DP = ("y", "z", "core")


def shifted(value, axis, by):
    size = lax.axis_size(axis)
    return lax.ppermute(value, axis, [(i, (i + by) % size) for i in range(size)])


def ring_scatter(block, size, axis):
    def pair(high, low):
        high, low = lax.optimization_barrier(
            (high.astype(jnp.bfloat16), low.astype(jnp.bfloat16))
        )
        high, low = shifted(high, axis, 1), shifted(low, axis, -1)
        return high.astype(jnp.float32), low.astype(jnp.float32)

    far = block(size // 2)
    half = far.shape[0] // 2
    up, down = pair(far[:half], far[half:])
    zero = jnp.zeros_like(up)
    up = jnp.concatenate([up, zero], axis=0)
    down = jnp.concatenate([zero, down], axis=0)
    for offset in range(size // 2 - 1, 0, -1):
        up, down = pair(block(offset) + up, block(-offset) + down)
    return block(0) + up + down


def spread(block, axis):
    size = lax.axis_size(axis)
    copies = jnp.broadcast_to(block[None], (size,) + block.shape)
    return lax.all_to_all(copies, axis, 0, 0, tiled=True)


SUMS = (("core", 1), ("z", 1), ("z", 2), ("z", 4), ("y", 1), ("y", 2))


def spread(block, axis):
    size = lax.axis_size(axis)
    copies = jnp.broadcast_to(block[None], (size,) + block.shape)
    return lax.all_to_all(copies, axis, 0, 0, tiled=True)


def gathered(shard, value):
    rows, width = shard.shape
    half = width // CORE
    chip = shard.reshape(rows, CORE, half).transpose(1, 0, 2)
    chip = lax.all_to_all(chip, "core", 0, 0, tiled=True).reshape(CORE * rows, half)
    column = spread(chip, "z").reshape(Z * CORE * rows, half)
    column, value = lax.optimization_barrier((column, value))
    own = spread(column, "y").reshape(Y * Z * CORE * rows, half)
    for name, bit in SUMS:
        pairs = [(i, i ^ bit) for i in range(lax.axis_size(name))]
        value = value + lax.ppermute(value, name, pairs)
    own, value = lax.optimization_barrier((own, value))
    return own, shifted(own, "core", 1), value


def swapped(blocks, axis):
    got = lax.all_to_all(blocks.astype(jnp.bfloat16), axis, 0, 0, tiled=True)
    total = got[0].astype(jnp.float32)
    for i in range(1, got.shape[0]):
        total = total + got[i].astype(jnp.float32)
    return total


def scattered(left, right):
    depth, cols = left.shape[1], right.shape[1]
    half = cols // 2
    unit = depth // (Y * Z)
    first = jnp.einsum("td,tk->dk", left, right[:, :half], preferred_element_type=jnp.float32)
    first = first.astype(jnp.bfloat16)
    later, first = lax.optimization_barrier((right[:, half:], first))
    first = swapped(first.reshape(Y, Z * unit, half), "y")
    second = jnp.einsum("td,tk->dk", left, later, preferred_element_type=jnp.float32)
    second = second.reshape(Y, Z, unit, half)
    here = lax.axis_index("z")

    def block(offset):
        piece = lax.dynamic_slice_in_dim(second, (here + offset) % Z, 1, 1)
        return piece.reshape(Y * unit, half)

    second = ring_scatter(block, Z, "z")
    first = swapped(first.reshape(Z, unit, half), "z")
    first, second = lax.optimization_barrier((first, second))
    second = swapped(second.reshape(Y, unit, half), "y")
    return jnp.concatenate([first, second], axis=1)


def local_statistics(proxy_loss, reference_loss, lengths, doc_domain):
    rows = proxy_loss.shape[0]
    ends = jnp.cumsum(lengths[0])
    position = jnp.arange(rows, dtype=jnp.int32)
    doc_index = jnp.sum((position[:, None] >= ends[None, :]).astype(jnp.int32), axis=1)
    doc_hot = doc_index[:, None] == jnp.arange(DOCS, dtype=jnp.int32)[None, :]
    end_of = jnp.sum(jnp.where(doc_hot, ends[None, :], 0), axis=1)
    live = position + 1 != end_of
    domain = jnp.sum(jnp.where(doc_hot, doc_domain[0][None, :], 0), axis=1)
    onehot = (domain[:, None] == jnp.arange(DOMAINS, dtype=jnp.int32)[None, :]).astype(jnp.float32)
    selected = (live & (proxy_loss > reference_loss)).astype(jnp.float32)
    excess = selected * (proxy_loss - reference_loss)
    excess_part = jnp.sum(onehot * excess[:, None], axis=0)
    count_part = jnp.sum(onehot * live.astype(jnp.float32)[:, None], axis=0)
    return (onehot, selected, excess_part, count_part)


def domain_weights(statistics, parts, log_weights, step_count, total_tokens):
    onehot, selected = statistics[:2]
    excess_sum, count = parts[0, :DOMAINS], parts[1, :DOMAINS]
    counts = jnp.maximum(count, 1.0)
    mean_excess = excess_sum / counts
    rate = 1.0 / jnp.sqrt(step_count[0].astype(jnp.float32))
    logits = log_weights + rate * mean_excess
    new_log = logits - jnp.log(jnp.sum(jnp.exp(logits)))
    lam = (1.0 - SMOOTH) * jnp.exp(new_log) + SMOOTH / DOMAINS
    per_domain = lam * total_tokens / counts
    weight = jnp.sum(onehot * per_domain[None, :], axis=1) * selected
    return (weight, new_log)


def forward_kernel(x_ref, r_ref, gamma_ref, own_ref, other_ref, normed_ref, slope_ref, hidden_ref):
    depth = x_ref.shape[1]
    step = min(STEP, depth)
    half = own_ref.shape[1]
    slope_ref[...] = jnp.zeros_like(slope_ref)

    @pl.loop(0, depth // step)
    def _(i):
        cols = pl.ds(pl.multiple_of(i * step, step), step)
        x = x_ref[:, cols].astype(jnp.float32)
        normed = (x * r_ref[...] * gamma_ref[:, cols]).astype(jnp.bfloat16)
        normed_ref[:, cols] = normed
        for at, ref in ((0, own_ref), (half, other_ref)):
            slope_ref[:, at : at + half] += jnp.dot(
                normed, ref[cols, :], preferred_element_type=jnp.float32
            )

    act = slope_ref[...]
    sig = jax.nn.sigmoid(act)
    hidden_ref[...] = (act * sig).astype(jnp.bfloat16)
    slope_ref[...] = sig * (1.0 + act * (1.0 - sig))


def forward(x, inverse, gamma, own, other):
    rows, depth = x.shape
    width = 2 * own.shape[1]
    spec = pl.BlockSpec(memory_space=pltpu.VMEM)
    return pl.pallas_call(
        forward_kernel,
        in_specs=[spec] * 5,
        out_specs=[spec] * 3,
        out_shape=[
            jax.ShapeDtypeStruct((rows, depth), jnp.bfloat16),
            jax.ShapeDtypeStruct((rows, width), jnp.float32),
            jax.ShapeDtypeStruct((rows, width), jnp.bfloat16),
        ],
        compiler_params=pltpu.CompilerParams(vmem_limit_bytes=VMEM_LIMIT),
        cost_estimate=pl.CostEstimate(
            flops=2 * rows * depth * width, bytes_accessed=2 * depth * width, transcendentals=0
        ),
        name="forward",
    )(x, inverse, gamma, own, other)


def tick_kernel(
    index_ref,
    section_ref,
    came_ref,
    top_ref,
    x_ref,
    r_ref,
    weight_ref,
    slope_ref,
    gamma_ref,
    own_ref,
    other_ref,
    old_dx_ref,
    old_wg_ref,
    old_wa_ref,
    out_ref,
    dx_ref,
    wg_ref,
    wa_ref,
    cot_ref,
    scaled_ref,
    dx_block,
    wg_block,
    wa_block,
    sems,
):
    block, depth = came_ref.shape
    half = own_ref.shape[1]
    index = index_ref[0]
    is_top = section_ref[0] == SECTIONS - 1

    @pl.when((index >= 0) & (index < MICRO))
    def _():
        rows = pl.ds(pl.multiple_of(index * block, block), block)

        @pl.when(is_top)
        def _():
            cot_ref[...] = top_ref[rows, :]

        @pl.when(jnp.logical_not(is_top))
        def _():
            cot_ref[...] = came_ref[...]

        weight = weight_ref[rows, :]
        wg_block[...] = (weight * cot_ref[...].astype(jnp.float32)).astype(jnp.bfloat16)
        wg_copy = pltpu.make_async_copy(wg_block, wg_ref.at[rows, :], sems.at[0])
        wg_copy.start()
        step = min(STEP_IN, depth)

        def into(i, total):
            cols = pl.ds(pl.multiple_of(i * step, step), step)
            cot = cot_ref[:, cols]
            sums = [
                jnp.dot(cot, ref[cols, :], preferred_element_type=jnp.float32)
                for ref in (own_ref, other_ref)
            ]
            return total + jnp.concatenate(sums, axis=1)

        grad_h = lax.fori_loop(
            0, depth // step, into, jnp.zeros((block, 2 * half), jnp.float32)
        )
        grad_a = grad_h * slope_ref[rows, :]
        wa_block[...] = (weight * grad_a).astype(jnp.bfloat16)
        wa_copy = pltpu.make_async_copy(wa_block, wa_ref.at[rows, :], sems.at[1])
        wa_copy.start()
        rounded = grad_a.astype(jnp.bfloat16)
        stride = min(STEP_OUT, depth)

        def back(i, dots):
            cols = pl.ds(pl.multiple_of(i * stride, stride), stride)
            grad_n = sum(
                lax.dot_general(
                    rounded[:, at : at + half],
                    ref[cols, :],
                    (((1,), (1,)), ((), ())),
                    preferred_element_type=jnp.float32,
                )
                for at, ref in ((0, own_ref), (half, other_ref))
            )
            scaled = gamma_ref[:, cols] * grad_n
            scaled_ref[:, cols] = scaled
            prod = x_ref[rows, cols].astype(jnp.float32) * scaled
            return dots + jnp.sum(prod, axis=1, keepdims=True)

        dots = lax.fori_loop(0, depth // stride, back, jnp.zeros((block, 1), jnp.float32))
        r = r_ref[rows, :]
        pull = r * r * r * (dots / depth)
        span = min(STEP_END, depth)

        @pl.loop(0, depth // span)
        def _(i):
            cols = pl.ds(pl.multiple_of(i * span, span), span)
            cot = cot_ref[:, cols].astype(jnp.float32)
            x = x_ref[rows, cols].astype(jnp.float32)
            passed = (cot + r * scaled_ref[:, cols] - x * pull).astype(jnp.bfloat16)
            out_ref[:, cols] = passed
            dx_block[:, cols] = (weight * passed.astype(jnp.float32)).astype(jnp.bfloat16)

        dx_copy = pltpu.make_async_copy(dx_block, dx_ref.at[rows, :], sems.at[2])
        dx_copy.start()
        wg_copy.wait()
        wa_copy.wait()
        dx_copy.wait()


def tick(index, section, came, top, x, inverse, weight, slope, gamma, own, other, dx, wg, wa):
    block, depth = came.shape
    width = slope.shape[1]
    spec = pl.BlockSpec(memory_space=pltpu.VMEM)
    scalar = pl.BlockSpec(memory_space=pltpu.SMEM)
    return pl.pallas_call(
        tick_kernel,
        in_specs=[scalar] * 2 + [spec] * 9 + [pl.BlockSpec(memory_space=pl.ANY)] * 3,
        out_specs=[spec] + [pl.BlockSpec(memory_space=pl.ANY)] * 3,
        scratch_shapes=[
            pltpu.VMEM((block, depth), jnp.bfloat16),
            pltpu.VMEM((block, depth), jnp.float32),
            pltpu.VMEM((block, depth), jnp.bfloat16),
            pltpu.VMEM((block, depth), jnp.bfloat16),
            pltpu.VMEM((block, width), jnp.bfloat16),
            pltpu.SemaphoreType.DMA((3,)),
        ],
        out_shape=[
            jax.ShapeDtypeStruct((block, depth), jnp.bfloat16),
            jax.ShapeDtypeStruct(dx.shape, dx.dtype),
            jax.ShapeDtypeStruct(wg.shape, wg.dtype),
            jax.ShapeDtypeStruct(wa.shape, wa.dtype),
        ],
        input_output_aliases={11: 1, 12: 2, 13: 3},
        compiler_params=pltpu.CompilerParams(vmem_limit_bytes=VMEM_LIMIT),
        cost_estimate=pl.CostEstimate(
            flops=4 * 128 * depth * width, bytes_accessed=2 * depth * width, transcendentals=0
        ),
        name="tick",
    )(index, section, came, top, x, inverse, weight, slope, gamma, own, other, dx, wg, wa)


def local(
    section_inputs,
    gains,
    value_weight,
    top_cotangent,
    proxy_loss,
    reference_loss,
    lengths,
    doc_domain,
    log_weights,
    step_count,
):
    sections = lax.axis_size("section")
    section = lax.axis_index("section").astype(jnp.int32)[None]
    devices = Y * Z * CORE
    x = section_inputs[0]
    shard = value_weight[0]
    rows, depth = x.shape
    width = shard.shape[1]
    block = rows // MICRO
    total_tokens = rows * devices
    statistics = local_statistics(proxy_loss, reference_loss, lengths, doc_domain)
    parts = jnp.zeros((8, 128), jnp.float32)
    parts = parts.at[0, :DOMAINS].set(statistics[2]).at[1, :DOMAINS].set(statistics[3])
    own, other, parts = gathered(shard, parts)
    weight, new_log = domain_weights(statistics, parts, log_weights, step_count, total_tokens)
    weight = weight[:, None]
    xfull = x.astype(jnp.float32)
    inverse = lax.rsqrt(jnp.mean(xfull * xfull, axis=1, keepdims=True) + EPS)
    normed, slope, hidden = forward(x, inverse, gains, own, other)
    dx = jnp.zeros((rows, depth), jnp.bfloat16)
    wg = jnp.zeros((rows, depth), jnp.bfloat16)
    wa = jnp.zeros((rows, width), jnp.bfloat16)
    sent = {}
    ticks = MICRO + LAG * (sections - 1)
    for slot in range(ticks):
        came = sent[slot - LAG] if slot >= LAG else jnp.zeros((block, depth), jnp.bfloat16)
        out, dx, wg, wa = tick(
            section + (slot - LAG * (sections - 1)) + (LAG - 1) * section,
            section,
            came,
            top_cotangent,
            x,
            inverse,
            weight,
            slope,
            gains,
            own,
            other,
            dx,
            wg,
            wa,
        )
        pairs = [
            (s, s - 1)
            for s in range(1, sections)
            if 0 <= slot - LAG * (sections - 1 - s) < MICRO
        ]
        if pairs:
            sent[slot] = lax.ppermute(out, "section", pairs)
    left = jnp.concatenate([normed, wg], axis=0)
    right = jnp.concatenate([wa, hidden], axis=0)
    left = jnp.concatenate([left, shifted(left, "core", 1)], axis=0)
    half = width // CORE
    right = jnp.concatenate([right[:, :half], shifted(right[:, half:], "core", 1)], axis=0)
    part = scattered(left, right) * (1.0 / devices)
    pieces = lax.all_to_all(part.reshape(CORE, -1, width // CORE), "core", 0, 0, tiled=True)
    grad_shard = pieces.transpose(1, 0, 2).reshape(shard.shape)
    return (dx[None], grad_shard[None], new_log)


def solution(mesh):
    grid = Mesh(mesh.devices.reshape(-1, Y, Z, CORE), ("section",) + DP)
    return jax.shard_map(
        local,
        mesh=grid,
        in_specs=(
            P("section", DP, None),
            P("section", None),
            P("section", DP, None),
            P(DP, None),
            P(DP),
            P(DP),
            P(DP, None),
            P(DP, None),
            P(),
            P(),
        ),
        out_specs=(P("section", DP, None), P("section", DP, None), P()),
        check_vma=False,
    )
```

```python
import jax
import jax.numpy as jnp
from jax import lax
from jax.experimental import pallas as pl
from jax.experimental.pallas import tpu as pltpu
from jax.sharding import Mesh
from jax.sharding import PartitionSpec as P

DOMAINS = 22
MICRO = 4
SECTIONS = 4
DOCS = 8


EPS = 1e-05
SMOOTH = 0.001
Y, Z, CORE = 4, 8, 2
STEP = 1024
STEP_IN = 2048
STEP_OUT = 2048
STEP_END = 512
LAG = 3
VMEM_LIMIT = 24 * 1024 * 1024


DP = ("y", "z", "core")


def shifted(value, axis, by):
    size = lax.axis_size(axis)
    return lax.ppermute(value, axis, [(i, (i + by) % size) for i in range(size)])


def summed(value):
    for axis in ("core", "z", "y"):
        size = lax.axis_size(axis)
        copies = jnp.broadcast_to(value[None], (size,) + value.shape)
        value = jnp.sum(lax.all_to_all(copies, axis, 0, 0, tiled=True), axis=0)
    return value


def ring_scatter(block, size, axis):
    def pair(high, low):
        high, low = lax.optimization_barrier(
            (high.astype(jnp.bfloat16), low.astype(jnp.bfloat16))
        )
        high, low = shifted(high, axis, 1), shifted(low, axis, -1)
        return high.astype(jnp.float32), low.astype(jnp.float32)

    far = block(size // 2)
    half = far.shape[0] // 2
    up, down = pair(far[:half], far[half:])
    zero = jnp.zeros_like(up)
    up = jnp.concatenate([up, zero], axis=0)
    down = jnp.concatenate([zero, down], axis=0)
    for offset in range(size // 2 - 1, 0, -1):
        up, down = pair(block(offset) + up, block(-offset) + down)
    return block(0) + up + down


def swapped(blocks, axis):
    got = lax.all_to_all(blocks.astype(jnp.bfloat16), axis, 0, 0, tiled=True)
    total = got[0].astype(jnp.float32)
    for i in range(1, got.shape[0]):
        total = total + got[i].astype(jnp.float32)
    return total


def scattered(left, right):
    depth, cols = left.shape[1], right.shape[1]
    cut = cols // 4
    unit = depth // (Y * Z)
    first = jnp.einsum("td,tk->dk", left, right[:, :cut], preferred_element_type=jnp.float32)
    first = first.astype(jnp.bfloat16)
    later, first = lax.optimization_barrier((right[:, cut:], first))
    first = swapped(first.reshape(Y, Z * unit, cut), "y")
    second = jnp.einsum("td,tk->dk", left, later, preferred_element_type=jnp.float32)
    second = second.reshape(Y, Z, unit, cols - cut)
    here = lax.axis_index("z")

    def block(offset):
        piece = lax.dynamic_slice_in_dim(second, (here + offset) % Z, 1, 1)
        return piece.reshape(Y * unit, cols - cut)

    second = ring_scatter(block, Z, "z")
    first = swapped(first.reshape(Z, unit, cut), "z")
    first, second = lax.optimization_barrier((first, second))
    second = swapped(second.reshape(Y, unit, cols - cut), "y")
    return jnp.concatenate([first, second], axis=1)


def local_statistics(proxy_loss, reference_loss, lengths, doc_domain):
    rows = proxy_loss.shape[0]
    ends = jnp.cumsum(lengths[0])
    position = jnp.arange(rows, dtype=jnp.int32)
    doc_index = jnp.sum((position[:, None] >= ends[None, :]).astype(jnp.int32), axis=1)
    doc_hot = doc_index[:, None] == jnp.arange(DOCS, dtype=jnp.int32)[None, :]
    end_of = jnp.sum(jnp.where(doc_hot, ends[None, :], 0), axis=1)
    live = position + 1 != end_of
    domain = jnp.sum(jnp.where(doc_hot, doc_domain[0][None, :], 0), axis=1)
    onehot = (domain[:, None] == jnp.arange(DOMAINS, dtype=jnp.int32)[None, :]).astype(jnp.float32)
    selected = (live & (proxy_loss > reference_loss)).astype(jnp.float32)
    excess = selected * (proxy_loss - reference_loss)
    excess_part = jnp.sum(onehot * excess[:, None], axis=0)
    count_part = jnp.sum(onehot * live.astype(jnp.float32)[:, None], axis=0)
    return (onehot, selected, excess_part, count_part)


def domain_weights(statistics, log_weights, step_count, total_tokens):
    onehot, selected, excess_part, count_part = statistics
    parts = jnp.zeros((8, 128), jnp.float32)
    parts = parts.at[0, :DOMAINS].set(excess_part).at[1, :DOMAINS].set(count_part)
    parts = summed(parts)
    excess_sum, count = parts[0, :DOMAINS], parts[1, :DOMAINS]
    counts = jnp.maximum(count, 1.0)
    mean_excess = excess_sum / counts
    rate = 1.0 / jnp.sqrt(step_count[0].astype(jnp.float32))
    logits = log_weights + rate * mean_excess
    new_log = logits - jnp.log(jnp.sum(jnp.exp(logits)))
    lam = (1.0 - SMOOTH) * jnp.exp(new_log) + SMOOTH / DOMAINS
    per_domain = lam * total_tokens / counts
    weight = jnp.sum(onehot * per_domain[None, :], axis=1) * selected
    return (weight, new_log)


def forward_kernel(x_ref, r_ref, gamma_ref, w_ref, normed_ref, slope_ref, hidden_ref):
    depth = x_ref.shape[1]
    step = min(STEP, depth)
    slope_ref[...] = jnp.zeros_like(slope_ref)

    @pl.loop(0, depth // step)
    def _(i):
        cols = pl.ds(pl.multiple_of(i * step, step), step)
        x = x_ref[:, cols].astype(jnp.float32)
        normed = (x * r_ref[...] * gamma_ref[:, cols]).astype(jnp.bfloat16)
        normed_ref[:, cols] = normed
        slope_ref[...] += jnp.dot(normed, w_ref[cols, :], preferred_element_type=jnp.float32)

    act = slope_ref[...]
    sig = jax.nn.sigmoid(act)
    hidden_ref[...] = (act * sig).astype(jnp.bfloat16)
    slope_ref[...] = sig * (1.0 + act * (1.0 - sig))


def forward(x, inverse, gamma, weight):
    rows, depth = x.shape
    width = weight.shape[1]
    spec = pl.BlockSpec(memory_space=pltpu.VMEM)
    return pl.pallas_call(
        forward_kernel,
        in_specs=[spec] * 4,
        out_specs=[spec] * 3,
        out_shape=[
            jax.ShapeDtypeStruct((rows, depth), jnp.bfloat16),
            jax.ShapeDtypeStruct((rows, width), jnp.float32),
            jax.ShapeDtypeStruct((rows, width), jnp.bfloat16),
        ],
        compiler_params=pltpu.CompilerParams(vmem_limit_bytes=VMEM_LIMIT),
        cost_estimate=pl.CostEstimate(
            flops=2 * rows * depth * width, bytes_accessed=2 * depth * width, transcendentals=0
        ),
        name="forward",
    )(x, inverse, gamma, weight)


def tick_kernel(
    index_ref,
    section_ref,
    came_ref,
    top_ref,
    x_ref,
    r_ref,
    weight_ref,
    slope_ref,
    gamma_ref,
    w_ref,
    old_dx_ref,
    old_wg_ref,
    old_wa_ref,
    out_ref,
    dx_ref,
    wg_ref,
    wa_ref,
    cot_ref,
    scaled_ref,
    dx_block,
    wg_block,
    wa_block,
    sems,
):
    block, depth = came_ref.shape
    index = index_ref[0]
    is_top = section_ref[0] == SECTIONS - 1

    @pl.when((index >= 0) & (index < MICRO))
    def _():
        rows = pl.ds(pl.multiple_of(index * block, block), block)

        @pl.when(is_top)
        def _():
            cot_ref[...] = top_ref[rows, :]

        @pl.when(jnp.logical_not(is_top))
        def _():
            cot_ref[...] = came_ref[...]

        weight = weight_ref[rows, :]
        wg_block[...] = (weight * cot_ref[...].astype(jnp.float32)).astype(jnp.bfloat16)
        wg_copy = pltpu.make_async_copy(wg_block, wg_ref.at[rows, :], sems.at[0])
        wg_copy.start()
        step = min(STEP_IN, depth)

        def into(i, total):
            cols = pl.ds(pl.multiple_of(i * step, step), step)
            return total + jnp.dot(
                cot_ref[:, cols], w_ref[cols, :], preferred_element_type=jnp.float32
            )

        grad_h = lax.fori_loop(
            0, depth // step, into, jnp.zeros((block, w_ref.shape[1]), jnp.float32)
        )
        grad_a = grad_h * slope_ref[rows, :]
        wa_block[...] = (weight * grad_a).astype(jnp.bfloat16)
        wa_copy = pltpu.make_async_copy(wa_block, wa_ref.at[rows, :], sems.at[1])
        wa_copy.start()
        rounded = grad_a.astype(jnp.bfloat16)
        stride = min(STEP_OUT, depth)

        def back(i, dots):
            cols = pl.ds(pl.multiple_of(i * stride, stride), stride)
            grad_n = lax.dot_general(
                rounded,
                w_ref[cols, :],
                (((1,), (1,)), ((), ())),
                preferred_element_type=jnp.float32,
            )
            scaled = gamma_ref[:, cols] * grad_n
            scaled_ref[:, cols] = scaled
            prod = x_ref[rows, cols].astype(jnp.float32) * scaled
            return dots + jnp.sum(prod, axis=1, keepdims=True)

        dots = lax.fori_loop(0, depth // stride, back, jnp.zeros((block, 1), jnp.float32))
        r = r_ref[rows, :]
        pull = r * r * r * (dots / depth)
        span = min(STEP_END, depth)

        @pl.loop(0, depth // span)
        def _(i):
            cols = pl.ds(pl.multiple_of(i * span, span), span)
            cot = cot_ref[:, cols].astype(jnp.float32)
            x = x_ref[rows, cols].astype(jnp.float32)
            passed = (cot + r * scaled_ref[:, cols] - x * pull).astype(jnp.bfloat16)
            out_ref[:, cols] = passed
            dx_block[:, cols] = (weight * passed.astype(jnp.float32)).astype(jnp.bfloat16)

        dx_copy = pltpu.make_async_copy(dx_block, dx_ref.at[rows, :], sems.at[2])
        dx_copy.start()
        wg_copy.wait()
        wa_copy.wait()
        dx_copy.wait()


def tick(index, section, came, top, x, inverse, weight, slope, gamma, w, dx, wg, wa):
    block, depth = came.shape
    width = slope.shape[1]
    spec = pl.BlockSpec(memory_space=pltpu.VMEM)
    scalar = pl.BlockSpec(memory_space=pltpu.SMEM)
    return pl.pallas_call(
        tick_kernel,
        in_specs=[scalar] * 2 + [spec] * 8 + [pl.BlockSpec(memory_space=pl.ANY)] * 3,
        out_specs=[spec] + [pl.BlockSpec(memory_space=pl.ANY)] * 3,
        scratch_shapes=[
            pltpu.VMEM((block, depth), jnp.bfloat16),
            pltpu.VMEM((block, depth), jnp.float32),
            pltpu.VMEM((block, depth), jnp.bfloat16),
            pltpu.VMEM((block, depth), jnp.bfloat16),
            pltpu.VMEM((block, width), jnp.bfloat16),
            pltpu.SemaphoreType.DMA((3,)),
        ],
        out_shape=[
            jax.ShapeDtypeStruct((block, depth), jnp.bfloat16),
            jax.ShapeDtypeStruct(dx.shape, dx.dtype),
            jax.ShapeDtypeStruct(wg.shape, wg.dtype),
            jax.ShapeDtypeStruct(wa.shape, wa.dtype),
        ],
        input_output_aliases={10: 1, 11: 2, 12: 3},
        compiler_params=pltpu.CompilerParams(vmem_limit_bytes=VMEM_LIMIT),
        cost_estimate=pl.CostEstimate(
            flops=4 * 128 * depth * width, bytes_accessed=2 * depth * width, transcendentals=0
        ),
        name="tick",
    )(index, section, came, top, x, inverse, weight, slope, gamma, w, dx, wg, wa)


def local(
    section_inputs,
    gains,
    value_weight,
    top_cotangent,
    proxy_loss,
    reference_loss,
    lengths,
    doc_domain,
    log_weights,
    step_count,
):
    sections = lax.axis_size("section")
    section = lax.axis_index("section").astype(jnp.int32)[None]
    devices = Y * Z * CORE
    core = lax.axis_index("core")
    x = section_inputs[0]
    shard = value_weight[0]
    rows, depth = x.shape
    width = shard.shape[1]
    block = rows // MICRO
    total_tokens = rows * devices
    statistics = local_statistics(proxy_loss, reference_loss, lengths, doc_domain)
    weight, new_log = domain_weights(statistics, log_weights, step_count, total_tokens)
    weight = weight[:, None]
    xfull = x.astype(jnp.float32)
    inverse = lax.rsqrt(jnp.mean(xfull * xfull, axis=1, keepdims=True) + EPS)
    inverse, weight = lax.optimization_barrier((inverse, weight))
    full_weight = lax.all_gather(shard, DP, axis=0, tiled=True)
    normed, slope, hidden = forward(x, inverse, gains, full_weight)
    dx = jnp.zeros((rows, depth), jnp.bfloat16)
    wg = jnp.zeros((rows, depth), jnp.bfloat16)
    wa = jnp.zeros((rows, width), jnp.bfloat16)
    sent = {}
    ticks = MICRO + LAG * (sections - 1)
    for slot in range(ticks):
        came = sent[slot - LAG] if slot >= LAG else jnp.zeros((block, depth), jnp.bfloat16)
        out, dx, wg, wa = tick(
            section + (slot - LAG * (sections - 1)) + (LAG - 1) * section,
            section,
            came,
            top_cotangent,
            x,
            inverse,
            weight,
            slope,
            gains,
            full_weight,
            dx,
            wg,
            wa,
        )
        pairs = [
            (s, s - 1)
            for s in range(1, sections)
            if 0 <= slot - LAG * (sections - 1 - s) < MICRO
        ]
        if pairs:
            sent[slot] = lax.ppermute(out, "section", pairs)
    left = jnp.concatenate([normed, wg], axis=0)
    right = jnp.concatenate([wa, hidden], axis=0)
    left = jnp.concatenate([left, shifted(left, "core", 1)], axis=0)
    halves = right.reshape(2 * rows, CORE, width // CORE).transpose(1, 0, 2)
    halves = lax.all_to_all(halves, "core", 0, 0, tiled=True)
    order = jnp.where(core == 0, halves, halves[::-1])
    right = order.reshape(CORE * 2 * rows, width // CORE)
    part = scattered(left, right) * (1.0 / devices)
    pieces = lax.all_to_all(part.reshape(CORE, -1, width // CORE), "core", 0, 0, tiled=True)
    grad_shard = pieces.transpose(1, 0, 2).reshape(shard.shape)
    return (dx[None], grad_shard[None], new_log)


def solution(mesh):
    grid = Mesh(mesh.devices.reshape(-1, Y, Z, CORE), ("section",) + DP)
    return jax.shard_map(
        local,
        mesh=grid,
        in_specs=(
            P("section", DP, None),
            P("section", None),
            P("section", DP, None),
            P(DP, None),
            P(DP),
            P(DP),
            P(DP, None),
            P(DP, None),
            P(),
            P(),
        ),
        out_specs=(P("section", DP, None), P("section", DP, None), P()),
        check_vma=False,
    )
```

```python
import jax
import jax.numpy as jnp
from jax import lax
from jax.experimental import pallas as pl
from jax.experimental.pallas import tpu as pltpu
from jax.sharding import Mesh
from jax.sharding import PartitionSpec as P

DOMAINS = 22
MICRO = 4
SECTIONS = 4
DOCS = 8


EPS = 1e-05
SMOOTH = 0.001
Y, Z, CORE = 4, 8, 2
STEP = 1024
STEP_IN = 4096
STEP_OUT = 4096
STEP_END = 512
LAG = 2
VMEM_LIMIT = 24 * 1024 * 1024


DP = ("y", "z", "core")


def shifted(value, axis, by):
    size = lax.axis_size(axis)
    return lax.ppermute(value, axis, [(i, (i + by) % size) for i in range(size)])


def summed(value):
    for axis in ("core", "z", "y"):
        size = lax.axis_size(axis)
        copies = jnp.broadcast_to(value[None], (size,) + value.shape)
        value = jnp.sum(lax.all_to_all(copies, axis, 0, 0, tiled=True), axis=0)
    return value


def ring_scatter(block, size, axis):
    def pair(high, low):
        high, low = lax.optimization_barrier(
            (high.astype(jnp.bfloat16), low.astype(jnp.bfloat16))
        )
        high, low = shifted(high, axis, 1), shifted(low, axis, -1)
        return high.astype(jnp.float32), low.astype(jnp.float32)

    far = block(size // 2)
    half = far.shape[0] // 2
    up, down = pair(far[:half], far[half:])
    zero = jnp.zeros_like(up)
    up = jnp.concatenate([up, zero], axis=0)
    down = jnp.concatenate([zero, down], axis=0)
    for offset in range(size // 2 - 1, 0, -1):
        up, down = pair(block(offset) + up, block(-offset) + down)
    return block(0) + up + down


def swapped(blocks, axis):
    got = lax.all_to_all(blocks.astype(jnp.bfloat16), axis, 0, 0, tiled=True)
    total = got[0].astype(jnp.float32)
    for i in range(1, got.shape[0]):
        total = total + got[i].astype(jnp.float32)
    return total


def scattered(left, right):
    depth, cols = left.shape[1], right.shape[1]
    cut = cols // 4
    unit = depth // (Y * Z)
    first = jnp.einsum("td,tk->dk", left, right[:, :cut], preferred_element_type=jnp.float32)
    first = first.astype(jnp.bfloat16)
    later, first = lax.optimization_barrier((right[:, cut:], first))
    first = swapped(first.reshape(Y, Z * unit, cut), "y")
    second = jnp.einsum("td,tk->dk", left, later, preferred_element_type=jnp.float32)
    second = second.reshape(Y, Z, unit, cols - cut)
    here = lax.axis_index("z")

    def block(offset):
        piece = lax.dynamic_slice_in_dim(second, (here + offset) % Z, 1, 1)
        return piece.reshape(Y * unit, cols - cut)

    second = ring_scatter(block, Z, "z")
    first = swapped(first.reshape(Z, unit, cut), "z")
    first, second = lax.optimization_barrier((first, second))
    second = swapped(second.reshape(Y, unit, cols - cut), "y")
    return jnp.concatenate([first, second], axis=1)


def local_statistics(proxy_loss, reference_loss, lengths, doc_domain):
    rows = proxy_loss.shape[0]
    ends = jnp.cumsum(lengths[0])
    position = jnp.arange(rows, dtype=jnp.int32)
    doc_index = jnp.sum((position[:, None] >= ends[None, :]).astype(jnp.int32), axis=1)
    doc_hot = doc_index[:, None] == jnp.arange(DOCS, dtype=jnp.int32)[None, :]
    end_of = jnp.sum(jnp.where(doc_hot, ends[None, :], 0), axis=1)
    live = position + 1 != end_of
    domain = jnp.sum(jnp.where(doc_hot, doc_domain[0][None, :], 0), axis=1)
    onehot = (domain[:, None] == jnp.arange(DOMAINS, dtype=jnp.int32)[None, :]).astype(jnp.float32)
    selected = (live & (proxy_loss > reference_loss)).astype(jnp.float32)
    excess = selected * (proxy_loss - reference_loss)
    excess_part = jnp.sum(onehot * excess[:, None], axis=0)
    count_part = jnp.sum(onehot * live.astype(jnp.float32)[:, None], axis=0)
    return (onehot, selected, excess_part, count_part)


def domain_weights(statistics, log_weights, step_count, total_tokens):
    onehot, selected, excess_part, count_part = statistics
    parts = jnp.zeros((8, 128), jnp.float32)
    parts = parts.at[0, :DOMAINS].set(excess_part).at[1, :DOMAINS].set(count_part)
    parts = summed(parts)
    excess_sum, count = parts[0, :DOMAINS], parts[1, :DOMAINS]
    counts = jnp.maximum(count, 1.0)
    mean_excess = excess_sum / counts
    rate = 1.0 / jnp.sqrt(step_count[0].astype(jnp.float32))
    logits = log_weights + rate * mean_excess
    new_log = logits - jnp.log(jnp.sum(jnp.exp(logits)))
    lam = (1.0 - SMOOTH) * jnp.exp(new_log) + SMOOTH / DOMAINS
    per_domain = lam * total_tokens / counts
    weight = jnp.sum(onehot * per_domain[None, :], axis=1) * selected
    return (weight, new_log)


def forward_kernel(x_ref, r_ref, gamma_ref, w_ref, normed_ref, slope_ref, hidden_ref):
    depth = x_ref.shape[1]
    step = min(STEP, depth)
    slope_ref[...] = jnp.zeros_like(slope_ref)

    @pl.loop(0, depth // step)
    def _(i):
        cols = pl.ds(pl.multiple_of(i * step, step), step)
        x = x_ref[:, cols].astype(jnp.float32)
        normed = (x * r_ref[...] * gamma_ref[:, cols]).astype(jnp.bfloat16)
        normed_ref[:, cols] = normed
        slope_ref[...] += jnp.dot(normed, w_ref[cols, :], preferred_element_type=jnp.float32)

    act = slope_ref[...]
    sig = jax.nn.sigmoid(act)
    hidden_ref[...] = (act * sig).astype(jnp.bfloat16)
    slope_ref[...] = sig * (1.0 + act * (1.0 - sig))


def forward(x, inverse, gamma, weight):
    rows, depth = x.shape
    width = weight.shape[1]
    spec = pl.BlockSpec(memory_space=pltpu.VMEM)
    return pl.pallas_call(
        forward_kernel,
        in_specs=[spec] * 4,
        out_specs=[spec] * 3,
        out_shape=[
            jax.ShapeDtypeStruct((rows, depth), jnp.bfloat16),
            jax.ShapeDtypeStruct((rows, width), jnp.float32),
            jax.ShapeDtypeStruct((rows, width), jnp.bfloat16),
        ],
        compiler_params=pltpu.CompilerParams(vmem_limit_bytes=VMEM_LIMIT),
        cost_estimate=pl.CostEstimate(
            flops=2 * rows * depth * width, bytes_accessed=2 * depth * width, transcendentals=0
        ),
        name="forward",
    )(x, inverse, gamma, weight)


def tick_kernel(
    index_ref,
    section_ref,
    came_ref,
    top_ref,
    x_ref,
    r_ref,
    weight_ref,
    slope_ref,
    gamma_ref,
    w_ref,
    old_dx_ref,
    old_wg_ref,
    old_wa_ref,
    out_ref,
    dx_ref,
    wg_ref,
    wa_ref,
    cot_ref,
    scaled_ref,
    dx_block,
    wg_block,
    wa_block,
    sems,
):
    block, depth = came_ref.shape
    index = index_ref[0]
    is_top = section_ref[0] == SECTIONS - 1

    @pl.when((index >= 0) & (index < MICRO))
    def _():
        rows = pl.ds(pl.multiple_of(index * block, block), block)

        @pl.when(is_top)
        def _():
            cot_ref[...] = top_ref[rows, :]

        @pl.when(jnp.logical_not(is_top))
        def _():
            cot_ref[...] = came_ref[...]

        weight = weight_ref[rows, :]
        wg_block[...] = (weight * cot_ref[...].astype(jnp.float32)).astype(jnp.bfloat16)
        wg_copy = pltpu.make_async_copy(wg_block, wg_ref.at[rows, :], sems.at[0])
        wg_copy.start()
        step = min(STEP_IN, depth)

        def into(i, total):
            cols = pl.ds(pl.multiple_of(i * step, step), step)
            return total + jnp.dot(
                cot_ref[:, cols], w_ref[cols, :], preferred_element_type=jnp.float32
            )

        grad_h = lax.fori_loop(
            0, depth // step, into, jnp.zeros((block, w_ref.shape[1]), jnp.float32)
        )
        grad_a = grad_h * slope_ref[rows, :]
        wa_block[...] = (weight * grad_a).astype(jnp.bfloat16)
        wa_copy = pltpu.make_async_copy(wa_block, wa_ref.at[rows, :], sems.at[1])
        wa_copy.start()
        rounded = grad_a.astype(jnp.bfloat16)
        stride = min(STEP_OUT, depth)

        def back(i, dots):
            cols = pl.ds(pl.multiple_of(i * stride, stride), stride)
            grad_n = lax.dot_general(
                rounded,
                w_ref[cols, :],
                (((1,), (1,)), ((), ())),
                preferred_element_type=jnp.float32,
            )
            scaled = gamma_ref[:, cols] * grad_n
            scaled_ref[:, cols] = scaled
            prod = x_ref[rows, cols].astype(jnp.float32) * scaled
            return dots + jnp.sum(prod, axis=1, keepdims=True)

        dots = lax.fori_loop(0, depth // stride, back, jnp.zeros((block, 1), jnp.float32))
        r = r_ref[rows, :]
        pull = r * r * r * (dots / depth)
        span = min(STEP_END, depth)

        @pl.loop(0, depth // span)
        def _(i):
            cols = pl.ds(pl.multiple_of(i * span, span), span)
            cot = cot_ref[:, cols].astype(jnp.float32)
            x = x_ref[rows, cols].astype(jnp.float32)
            passed = (cot + r * scaled_ref[:, cols] - x * pull).astype(jnp.bfloat16)
            out_ref[:, cols] = passed
            dx_block[:, cols] = (weight * passed.astype(jnp.float32)).astype(jnp.bfloat16)

        dx_copy = pltpu.make_async_copy(dx_block, dx_ref.at[rows, :], sems.at[2])
        dx_copy.start()
        wg_copy.wait()
        wa_copy.wait()
        dx_copy.wait()


def tick(index, section, came, top, x, inverse, weight, slope, gamma, w, dx, wg, wa):
    block, depth = came.shape
    width = slope.shape[1]
    spec = pl.BlockSpec(memory_space=pltpu.VMEM)
    scalar = pl.BlockSpec(memory_space=pltpu.SMEM)
    return pl.pallas_call(
        tick_kernel,
        in_specs=[scalar] * 2 + [spec] * 8 + [pl.BlockSpec(memory_space=pl.ANY)] * 3,
        out_specs=[spec] + [pl.BlockSpec(memory_space=pl.ANY)] * 3,
        scratch_shapes=[
            pltpu.VMEM((block, depth), jnp.bfloat16),
            pltpu.VMEM((block, depth), jnp.float32),
            pltpu.VMEM((block, depth), jnp.bfloat16),
            pltpu.VMEM((block, depth), jnp.bfloat16),
            pltpu.VMEM((block, width), jnp.bfloat16),
            pltpu.SemaphoreType.DMA((3,)),
        ],
        out_shape=[
            jax.ShapeDtypeStruct((block, depth), jnp.bfloat16),
            jax.ShapeDtypeStruct(dx.shape, dx.dtype),
            jax.ShapeDtypeStruct(wg.shape, wg.dtype),
            jax.ShapeDtypeStruct(wa.shape, wa.dtype),
        ],
        input_output_aliases={10: 1, 11: 2, 12: 3},
        compiler_params=pltpu.CompilerParams(vmem_limit_bytes=VMEM_LIMIT),
        cost_estimate=pl.CostEstimate(
            flops=4 * 128 * depth * width, bytes_accessed=2 * depth * width, transcendentals=0
        ),
        name="tick",
    )(index, section, came, top, x, inverse, weight, slope, gamma, w, dx, wg, wa)


def local(
    section_inputs,
    gains,
    value_weight,
    top_cotangent,
    proxy_loss,
    reference_loss,
    lengths,
    doc_domain,
    log_weights,
    step_count,
):
    sections = lax.axis_size("section")
    section = lax.axis_index("section").astype(jnp.int32)[None]
    devices = Y * Z * CORE
    core = lax.axis_index("core")
    x = section_inputs[0]
    shard = value_weight[0]
    rows, depth = x.shape
    width = shard.shape[1]
    block = rows // MICRO
    total_tokens = rows * devices
    statistics = local_statistics(proxy_loss, reference_loss, lengths, doc_domain)
    weight, new_log = domain_weights(statistics, log_weights, step_count, total_tokens)
    weight = weight[:, None]
    xfull = x.astype(jnp.float32)
    inverse = lax.rsqrt(jnp.mean(xfull * xfull, axis=1, keepdims=True) + EPS)
    inverse, weight = lax.optimization_barrier((inverse, weight))
    full_weight = lax.all_gather(shard, DP, axis=0, tiled=True)
    normed, slope, hidden = forward(x, inverse, gains, full_weight)
    dx = jnp.zeros((rows, depth), jnp.bfloat16)
    wg = jnp.zeros((rows, depth), jnp.bfloat16)
    wa = jnp.zeros((rows, width), jnp.bfloat16)
    sent = {}
    ticks = MICRO + LAG * (sections - 1)
    for slot in range(ticks):
        came = sent[slot - LAG] if slot >= LAG else jnp.zeros((block, depth), jnp.bfloat16)
        out, dx, wg, wa = tick(
            section + (slot - LAG * (sections - 1)) + (LAG - 1) * section,
            section,
            came,
            top_cotangent,
            x,
            inverse,
            weight,
            slope,
            gains,
            full_weight,
            dx,
            wg,
            wa,
        )
        pairs = [
            (s, s - 1)
            for s in range(1, sections)
            if 0 <= slot - LAG * (sections - 1 - s) < MICRO
        ]
        if pairs:
            sent[slot] = lax.ppermute(out, "section", pairs)
    left = jnp.concatenate([normed, wg], axis=0)
    right = jnp.concatenate([wa, hidden], axis=0)
    left = jnp.concatenate([left, shifted(left, "core", 1)], axis=0)
    halves = right.reshape(2 * rows, CORE, width // CORE).transpose(1, 0, 2)
    halves = lax.all_to_all(halves, "core", 0, 0, tiled=True)
    order = jnp.where(core == 0, halves, halves[::-1])
    right = order.reshape(CORE * 2 * rows, width // CORE)
    part = scattered(left, right) * (1.0 / devices)
    pieces = lax.all_to_all(part.reshape(CORE, -1, width // CORE), "core", 0, 0, tiled=True)
    grad_shard = pieces.transpose(1, 0, 2).reshape(shard.shape)
    return (dx[None], grad_shard[None], new_log)


def solution(mesh):
    grid = Mesh(mesh.devices.reshape(-1, Y, Z, CORE), ("section",) + DP)
    return jax.shard_map(
        local,
        mesh=grid,
        in_specs=(
            P("section", DP, None),
            P("section", None),
            P("section", DP, None),
            P(DP, None),
            P(DP),
            P(DP),
            P(DP, None),
            P(DP, None),
            P(),
            P(),
        ),
        out_specs=(P("section", DP, None), P("section", DP, None), P()),
        check_vma=False,
    )
```
